32 devices in a mesh: job: 2 (over y), blk: 4 (over z), cell: 2 (over x), col: 2 (over core).
Axes of the slice: x: 2, y: 2, z: 4, core: 2. Of those that a mesh axis runs over, the one named last changes fastest.
Arguments:
- p_blocks: bfloat16 [64, 4, 2, 128, 128], P(('job', 'blk', 'cell')), parts along dimension 0, may hold values from -0.1875 to 0.1875
- p_cols: int32 [64, 4, 2], P(('job', 'blk', 'cell')), parts along dimension 0, may hold values from 0 to 7
- l_blocks: bfloat16 [64, 4, 2, 128, 128], P(('job', 'blk', 'cell')), parts along dimension 0, may hold values from -0.1875 to 0.1875
- l_cols: int32 [64, 4, 2], P(('job', 'blk', 'cell')), parts along dimension 0, may hold values from 0 to 7
- charges: bfloat16 [24, 2, 8192], P('col', None, ('job', 'blk', 'cell')), parts along dimension 2, may hold values from -6 to 6
- currents: bfloat16 [24, 2, 8192], P('col', None, ('job', 'blk', 'cell')), parts along dimension 2, may hold values from -6 to 6
- omegas: float32 [24], P('col'), may hold values from 0.5 to 4
- resist: float32 [8192], P(('job', 'blk', 'cell')), parts along dimension 0, may hold values from 0.05 to 2
- branch_ends: int32 [2, 8192], P(None, ('job', 'blk', 'cell')), parts along dimension 1, may hold values from 0 to 1023
Outputs:
- cell_rows: float32 [24, 2, 8192], P('col', None, ('job', 'blk', 'cell')), parts along dimension 2
- panel_rows: float32 [24, 2, 8192], P('col', None, ('job', 'blk', 'cell')), parts along dimension 2
The draws below stay inside these ranges and needn't reach their ends.
There are 2 independent parts, one for each index of `job`. The reference program is written for one: setup_inputs(seed, part) draws one part's arguments, and reference() takes and returns one part's arrays. A program takes and returns all parts, laid end to end along the dimension named above; an argument that names none is the same for every part. Nothing has to cross between parts.
Inputs may be any that keep to these rules, and one draw needn't show every extreme that they name: `p_cols`: block columns are numbered within the region of 8 blocks that the slot's region index names; repeats may occur. `l_cols`: as for p_cols. `branch_ends`: panel numbers within the cell's own region of 1024 panels; a cell may leave and enter the same panel.
All inputs are finite; a program needn't handle non-finite values.
Results may differ from the reference program's by a relative error of at most 0.0059.
Values may be sent and summed in bfloat16 or wider, within the bound.
A program may use at most 64 MiB of HBM per device.

```python
import math
import jax
import jax.numpy as jnp
from jax import lax

FREQS = 24
BS = 128
KP = 2
KL = 2
REG_BLOCKS = 8
REGION = 1024
NBLOCKS = 32
PANELS = 4096
CELLS = 4096
N_BLK = 4


def place_ends(values, own_key, smallest, largest):
    place = [jax.random.randint(jax.random.fold_in(own_key, axis), (), 0, length) for axis, length in enumerate(values.shape)]
    widest = values.shape.index(max(values.shape))
    beside = place[:widest] + [(place[widest] + 1) % values.shape[widest]] + place[widest + 1:]
    return values.at[tuple(place)].set(smallest).at[tuple(beside)].set(largest)


def levels(own_key, dims, split, low, largest):
    gain = 1.0
    for position, shards_of in split:
        draws = jax.random.uniform(jax.random.fold_in(jax.random.fold_in(own_key, 6), position), (shards_of,), jnp.float32, low / len(split), largest / len(split))
        gain = gain * jnp.repeat(jnp.exp(draws), dims[position] // shards_of).reshape((-1,) + (1,) * (len(dims) - 1 - position))
    return gain


def normal_values(stream_key, shape, deviation, bound, pieces=(), kind=jnp.bfloat16):
    level = levels(stream_key, shape, pieces, -0.22, 0.18) if pieces else 1.0
    array = jax.random.normal(stream_key, shape, jnp.float32) * deviation * level
    return jnp.minimum(jnp.maximum(array, -bound), bound).astype(kind)


def setup_inputs(seed: int = 0, part: int = 0) -> dict:
    seeds = jax.random.split(jax.random.key(seed), 10)
    own_keys = jax.random.split(jax.random.fold_in(seeds[9], part), 10)
    return {
        "p_blocks": normal_values(own_keys[0], (NBLOCKS, N_BLK, KP, BS, BS), (N_BLK * KP * BS) ** -0.5, 0.1875, ((0, 8),)),
        "p_cols": place_ends(jax.random.randint(own_keys[1], (NBLOCKS, N_BLK, KP), 0, REG_BLOCKS), jax.random.fold_in(own_keys[1], 1), 0, REG_BLOCKS - 1).astype(jnp.int32),
        "l_blocks": normal_values(own_keys[2], (NBLOCKS, N_BLK, KL, BS, BS), (N_BLK * KL * BS) ** -0.5, 0.1875, ((0, 8),)),
        "l_cols": place_ends(jax.random.randint(own_keys[3], (NBLOCKS, N_BLK, KL), 0, REG_BLOCKS), jax.random.fold_in(own_keys[3], 1), 0, REG_BLOCKS - 1).astype(jnp.int32),
        "charges": normal_values(own_keys[4], (FREQS, 2, PANELS), 1.0, 6.0, ((0, 2), (2, 8))),
        "currents": normal_values(own_keys[5], (FREQS, 2, CELLS), 1.0, 6.0, ((0, 2), (2, 8))),
        "omegas": jnp.clip(jnp.exp(math.log(4.0) - 2.0794415 * jax.random.uniform(seeds[6], (FREQS,), jnp.float32) ** levels(seeds[6], (FREQS,), ((0, 2),), -0.2, 0.2)), 0.5, 4.0),
        "resist": jnp.clip(jnp.exp(math.log(2.0) - 3.6888794 * jax.random.uniform(own_keys[7], (CELLS,), jnp.float32) ** levels(own_keys[7], (CELLS,), ((0, 8),), -0.2, 0.2)), 0.05, 2.0),
        "branch_ends": place_ends(jax.random.randint(own_keys[8], (2, CELLS), 0, REGION), jax.random.fold_in(own_keys[8], 1), 0, REGION - 1).astype(jnp.int32),
    }


def block_product(slabs, columns, vectors, reg_blocks):
    shifts = jnp.arange(N_BLK, dtype=jnp.int32)[:, None] * reg_blocks

    def one_row(pair):
        slab, index_set = pair
        picked_cols = (index_set.astype(jnp.int32) + shifts).astype(jnp.int32)
        picked = vectors[:, picked_cols].astype(jnp.float32)
        return jnp.einsum('skab,fskb->fa', slab.astype(jnp.float32), picked)

    result = lax.map(one_row, (slabs, columns))
    return jnp.transpose(result, (1, 0, 2)).reshape(result.shape[1], -1)


def reference(p_blocks, p_cols, l_blocks, l_cols, charges, currents, omegas, resist, branch_ends):
    col_rows = 2 * FREQS
    charge_mat = charges.reshape(col_rows, -1, BS)
    current_mat = currents.reshape(col_rows, -1, BS)
    potential = block_product(p_blocks, p_cols, charge_mat, REG_BLOCKS).astype(jnp.bfloat16)
    flux = block_product(l_blocks, l_cols, current_mat, REG_BLOCKS).reshape(FREQS, 2, -1)
    base = (jnp.arange(CELLS, dtype=jnp.int32) // REGION) * REGION
    source = (branch_ends[0] + base).astype(jnp.int32)
    target = (branch_ends[1] + base).astype(jnp.int32)
    drop = potential[:, source].astype(jnp.float32) - potential[:, target].astype(jnp.float32)
    drop = drop.reshape(FREQS, 2, -1)
    current_f = currents.astype(jnp.float32)
    scale = omegas[:, None]
    cell_re = resist * current_f[:, 0] - scale * flux[:, 1] + drop[:, 0]
    cell_im = resist * current_f[:, 1] + scale * flux[:, 0] + drop[:, 1]
    cell_rows = jnp.stack([cell_re, cell_im], axis=1)
    flat_cur = current_f.reshape(col_rows, -1).T
    outflow = jax.ops.segment_sum(flat_cur, source, PANELS) - jax.ops.segment_sum(flat_cur, target, PANELS)
    outflow = outflow.T.reshape(FREQS, 2, -1)
    charge_f = charges.astype(jnp.float32)
    panel_re = outflow[:, 0] - scale * charge_f[:, 1]
    panel_im = outflow[:, 1] + scale * charge_f[:, 0]
    panel_rows = jnp.stack([panel_re, panel_im], axis=1)
    return (cell_rows, panel_rows)
```

```python
import functools

import jax
import jax.numpy as jnp
from jax import lax
from jax.experimental import pallas as pl
from jax.experimental.pallas import tpu as pltpu
from jax.sharding import PartitionSpec as P

MESH = pl.DeviceIdType.MESH
NT = (((1,), (1,)), ((), ()))
NN = (((1,), (0,)), ((), ()))


def dot(a, b, dims):
    return lax.dot_general(a, b, dims, preferred_element_type=jnp.float32)


def quarter_turn(x):
    rows = x.shape[0]
    even = lax.broadcasted_iota(jnp.int32, x.shape, 0) % 2 == 0
    return jnp.where(even, -pltpu.roll(x, rows - 1, 0), pltpu.roll(x, 1, 0))


def kernel(n_blk, n_cell, *refs):
    (charges, currents, ends_hbm, resist_hbm, omegas_hbm, p_cols, l_cols, p_blocks, l_blocks,
     both, arr, mat, own_q, own_i, ends, resist, omegas, cols, blocks, acc, inc, flux,
     phi_out, phi_in, part_out, part_in, load_sem, send_sem, recv_sem, flux_sem,
     phi_send, phi_recv, part_send, part_recv, ready) = refs
    cell_out, panel_out = both.at[0], both.at[1]
    freqs, local = own_q.shape[0], own_q.shape[1]
    rows, share = 2 * freqs, local * 128
    z, x, c = lax.axis_index("blk"), lax.axis_index("cell"), lax.axis_index("col")
    hops = range(1, n_cell)

    def beside(dx):
        return lax.rem(x + dx, n_cell)

    def layer(zz):
        return [(zz, beside(dx), k) for dx in range(n_cell) for k in range(2)]

    def device(zz, xx, cc):
        return {"blk": zz, "cell": xx, "col": cc}

    barrier = pltpu.get_barrier_semaphore()

    def greet(zz, sem):
        for who in layer(zz):
            pl.semaphore_signal(sem, device_id=device(*who), device_id_type=MESH)

    for dx in range(n_cell):
        for dc in range(2):
            if dx or dc:
                pl.semaphore_signal(
                    barrier, device_id=device(z, beside(dx), lax.rem(c + dc, 2)), device_id_type=MESH)

    def greet_above(zz, carry):
        greet(zz, barrier)
        return carry

    lax.fori_loop(z + 1, n_blk, greet_above, 0)

    def load(i, src, dst):
        return pltpu.make_async_copy(src, dst, load_sem.at[i])

    mine = arr.at[z, x, c]
    loads = [
        load(0, charges, own_q), load(1, currents, own_i), load(2, ends_hbm, ends),
        load(3, resist_hbm, resist), load(4, omegas_hbm, omegas),
    ]
    role_1 = [load(5, charges, mine), load(6, p_cols, cols), load(7, p_blocks, blocks)]
    role_0 = [load(5, currents, mine), load(6, l_cols, cols), load(7, l_blocks, blocks)]

    pl.semaphore_wait(barrier, 2 * n_cell * (z + 1) - 1)

    def copy(kind, zz, xx):
        return pltpu.make_async_remote_copy(
            src_ref=(currents, charges)[kind], dst_ref=mine,
            send_sem=send_sem.at[kind, zz, xx], recv_sem=recv_sem.at[z, x, c],
            device_id=device(zz, xx, kind), device_id_type=MESH)

    def send(kind, zz):
        for dx in range(n_cell):
            copy(kind, zz, beside(dx)).start()

    def send_beside(kind):
        for dx in hops:
            copy(kind, z, beside(dx)).start()
        pl.when(c != kind)(lambda: copy(kind, z, x).start())

    def send_down(kind):
        def step(zz, carry):
            send(kind, zz)
            return carry

        lax.fori_loop(0, z, step, 0)

    send_down(1)

    def answer(zz, carry):
        greet(zz, ready.at[z])
        return carry

    lax.fori_loop(0, z, answer, 0)
    send_beside(1)
    for one in loads:
        one.start()

    @pl.when(c == 1)
    def _():
        for one in role_1:
            one.start()

    @pl.when(c == 0)
    def _():
        for one in role_0:
            one.start()

    send_down(0)
    send_beside(0)

    for one in loads:
        one.wait()

    def flat(ref):
        return jnp.concatenate(
            [ref[:, j].astype(jnp.float32).reshape(rows, 128) for j in range(local)], axis=1)

    i32 = flat(own_i)
    i16 = i32.astype(jnp.bfloat16)
    start = ends[0:1, :]
    stop = ends[1:2, :]
    chunk = 128
    base = lax.broadcasted_iota(jnp.int32, (chunk, share), 0)

    def fill(t, carry):
        offset = pl.multiple_of(t * chunk, chunk)
        plus = jnp.where(base == start - offset, 1.0, 0.0)
        minus = jnp.where(base == stop - offset, 1.0, 0.0)
        inc[pl.ds(offset, chunk), :] = (plus - minus).astype(jnp.bfloat16)
        return carry

    lax.fori_loop(0, n_cell * share // chunk, fill, 0)

    def inc_of(owner):
        return inc[pl.ds(pl.multiple_of(owner * share, share), share), :]

    def part_copy(dx):
        return pltpu.make_async_remote_copy(
            src_ref=part_out.at[dx], dst_ref=part_in.at[dx],
            send_sem=part_send.at[dx], recv_sem=part_recv.at[dx],
            device_id={"cell": beside(dx)}, device_id_type=MESH)

    for dx in hops:
        part_out[dx] = dot(i16, inc_of(beside(dx)), NT).astype(jnp.bfloat16)
        part_copy(dx).start()

    def send_up(zz, carry):
        pl.semaphore_wait(ready.at[zz], 2 * n_cell)
        send(1, zz)
        send(0, zz)
        return carry

    lax.fori_loop(z + 1, n_blk, send_up, 0)

    outflow = dot(i16, inc_of(x), NT)
    row = lax.broadcasted_iota(jnp.int32, (rows, 128), 0) // 2
    omega = jnp.zeros((rows, 128), jnp.float32)
    for f in range(freqs):
        omega = jnp.where(row == f, omegas[f], omega)
    omega = jnp.concatenate([omega] * local, axis=1)
    panel = outflow + omega * quarter_turn(flat(own_q))

    def wait_piece(zz, xx, cc):
        pltpu.make_async_remote_copy(
            src_ref=charges, dst_ref=arr.at[zz, xx, cc],
            send_sem=send_sem.at[0, zz, xx], recv_sem=recv_sem.at[zz, xx, cc],
            device_id=device(zz, xx, cc), device_id_type=MESH).wait_recv()

    def products(zz, first):
        for xx in range(n_cell):
            for j in range(local):
                mat[zz, xx * local + j] = arr[zz, xx, :, :, j].reshape(2 * rows, 128)
        for r in range(local):
            left = jnp.concatenate([mat[zz, cols[r, k, zz]] for k in range(2)], axis=1)
            right = jnp.concatenate([blocks[r, zz, k] for k in range(2)], axis=1)
            term = dot(left, right, NT)
            if first:
                acc[r] = term
            else:
                acc[r] += term

    for i in (5, 6, 7):
        role_1[i - 5].wait()
    for dx in range(n_cell):
        for dc in range(2):
            if dx or dc:
                wait_piece(z, beside(dx), lax.rem(c + dc, 2))
    products(z, True)

    below, above = z, n_blk - 1 - z
    paired = jnp.minimum(below, above)

    def arrive(i, carry):
        near = lax.div(i + 1, 2)
        far = i - paired
        two_sided = i <= 2 * paired
        dist = jnp.where(two_sided, near, far)
        down = jnp.where(two_sided, lax.rem(i, 2) == 1, below > above)
        zz = jnp.where(down, z - dist, z + dist)
        for xx in range(n_cell):
            for cc in range(2):
                wait_piece(zz, xx, cc)
        products(zz, False)
        return carry

    lax.fori_loop(1, n_blk, arrive, 0)

    flux_out = acc.at[:, pl.ds(rows, rows)]

    def flux_copy():
        return pltpu.make_async_remote_copy(
            src_ref=flux_out, dst_ref=flux, send_sem=flux_sem.at[0], recv_sem=flux_sem.at[1],
            device_id={"col": 1}, device_id_type=MESH)

    def phi_copy(dx, cc):
        return pltpu.make_async_remote_copy(
            src_ref=phi_out.at[cc], dst_ref=phi_in.at[x],
            send_sem=phi_send.at[dx, cc], recv_sem=phi_recv.at[x],
            device_id={"cell": beside(dx), "col": cc}, device_id_type=MESH)

    def wait_phi(xx):
        pltpu.make_async_remote_copy(
            src_ref=phi_out.at[0], dst_ref=phi_in.at[xx],
            send_sem=phi_send.at[0, 0], recv_sem=phi_recv.at[xx],
            device_id={"cell": xx}, device_id_type=MESH).wait_recv()

    @pl.when(c == 1)
    def _():
        phi = jnp.concatenate([acc[r] for r in range(local)], axis=1)
        phi_out[0] = phi[:rows].astype(jnp.bfloat16)
        for dx in hops:
            phi_copy(dx, 0).start()
        phi_out[1] = phi[rows:].astype(jnp.bfloat16)
        for dx in hops:
            phi_copy(dx, 1).start()
        phi_copy(0, 0).start()
        phi_in[x] = phi[rows:].astype(jnp.bfloat16)

    @pl.when(c == 0)
    def _():
        flux_copy().start()
        for r in range(local):
            flux[r] = acc[r, :rows]

    for dx in hops:
        part_copy(dx).wait_recv()
        panel += part_in[dx].astype(jnp.float32)
    panel_out[...] = panel.reshape(panel_out.shape)

    @pl.when(c == 1)
    def _():
        flux_copy().wait_recv()

    turned = quarter_turn(jnp.concatenate([flux[r] for r in range(local)], axis=1))
    cell = resist[...] * i32 + omega * turned

    @pl.when(c == 0)
    def _():
        wait_phi(x)

    cell += dot(phi_in[x], inc_of(x), NN)
    for dx in hops:
        wait_phi(beside(dx))
        cell += dot(phi_in[beside(dx)], inc_of(beside(dx)), NN)
    cell_out[...] = cell.reshape(cell_out.shape)

    for dx in hops:
        part_copy(dx).wait_send()

    @pl.when(c == 1)
    def _():
        phi_copy(0, 0).wait_send()
        for dx in hops:
            phi_copy(dx, 0).wait_send()
            phi_copy(dx, 1).wait_send()

    @pl.when(c == 0)
    def _():
        flux_copy().wait_send()

    def sent(zz, carry):
        for kind in (0, 1):
            for dx in range(n_cell):
                copy(kind, zz, beside(dx)).wait_send()
        return carry

    lax.fori_loop(0, z, sent, 0)
    lax.fori_loop(z + 1, n_blk, sent, 0)
    for kind in (0, 1):
        for dx in hops:
            copy(kind, z, beside(dx)).wait_send()
        pl.when(c != kind)(lambda kind=kind: copy(kind, z, x).wait_send())


def per_device(p_blocks, p_cols, l_blocks, l_cols, charges, currents, omegas, resist, branch_ends):
    n_blk, n_cell = lax.axis_size("blk"), lax.axis_size("cell")
    freqs, _, share = charges.shape
    rows, local = 2 * freqs, share // 128
    vmem, dma = pltpu.VMEM, pltpu.SemaphoreType.DMA

    def by_block(v):
        return v.reshape(freqs, 2, local, 128).transpose(0, 2, 1, 3)

    operands = (
        by_block(charges), by_block(currents), branch_ends, resist.reshape(1, share), omegas,
        p_cols.transpose(0, 2, 1), l_cols.transpose(0, 2, 1), p_blocks, l_blocks,
    )
    own = (freqs, local, 2, 128)
    bf16, f32 = jnp.bfloat16, jnp.float32
    outs = pl.pallas_call(
        functools.partial(kernel, n_blk, n_cell),
        out_shape=pltpu.VMEM((2, freqs, 2, share), f32),
        in_specs=[pl.BlockSpec(memory_space=pltpu.HBM)] * len(operands),
        out_specs=pl.BlockSpec(memory_space=vmem),
        scratch_shapes=[
            vmem((n_blk, n_cell, 2) + own, bf16),
            vmem((n_blk, n_cell * local, 2 * rows, 128), bf16),
            vmem(own, bf16),
            vmem(own, bf16),
            vmem(branch_ends.shape, jnp.int32),
            vmem((1, share), f32),
            pltpu.SMEM(omegas.shape, f32),
            pltpu.SMEM((local, 2, n_blk), jnp.int32),
            vmem(p_blocks.shape, bf16),
            vmem((local, 2 * rows, 128), f32),
            vmem((n_cell * share, share), bf16),
            vmem((local, rows, 128), f32),
            vmem((2, rows, share), bf16),
            vmem((n_cell, rows, share), bf16),
            vmem((n_cell, rows, share), bf16),
            vmem((n_cell, rows, share), bf16),
            dma((8,)),
            dma((2, n_blk, n_cell)),
            dma((n_blk, n_cell, 2)),
            dma((2,)),
            dma((n_cell, 2)),
            dma((n_cell,)),
            dma((n_cell,)),
            dma((n_cell,)),
            pltpu.SemaphoreType.REGULAR((n_blk,)),
        ],
        compiler_params=pltpu.CompilerParams(
            collective_id=0, has_side_effects=True, vmem_limit_bytes=60 * 2**20
        ),
    )(*[pltpu.with_memory_space_constraint(v, pltpu.HBM) for v in operands])
    return outs[0], outs[1]


def solution(mesh):
    across = ("job", "blk", "cell")
    placed = (
        P(across, None, None, None, None),
        P(across, None, None),
        P(across, None, None, None, None),
        P(across, None, None),
        P("col", None, across),
        P("col", None, across),
        P("col"),
        P(across),
        P(None, across),
    )
    return jax.shard_map(
        per_device,
        mesh=mesh,
        in_specs=placed,
        out_specs=(P("col", None, across), P("col", None, across)),
        check_vma=False,
    )
```

```python
import functools

import jax
import jax.numpy as jnp
from jax import lax
from jax.experimental import pallas as pl
from jax.experimental.pallas import tpu as pltpu
from jax.sharding import PartitionSpec as P

MESH = pl.DeviceIdType.MESH
NT = (((1,), (1,)), ((), ()))
NN = (((1,), (0,)), ((), ()))


def dot(a, b, dims):
    return lax.dot_general(a, b, dims, preferred_element_type=jnp.float32)


def quarter_turn(x):
    rows = x.shape[0]
    even = lax.broadcasted_iota(jnp.int32, x.shape, 0) % 2 == 0
    return jnp.where(even, -pltpu.roll(x, rows - 1, 0), pltpu.roll(x, 1, 0))


def kernel(n_blk, n_cell, *refs):
    (charges, currents, ends_hbm, resist_hbm, omegas_hbm, p_cols, l_cols, p_blocks, l_blocks,
     both, a_arr, b_arr, a_mat, b_mat, own_q, own_i, ends, resist, omegas, a_cols, b_cols,
     a_blocks, b_blocks, a_acc, b_acc, inc, phi_out, phi_in, part_out, part_in, load_sem,
     a_send, a_recv, a_pass, b_send, b_recv, b_pass, phi_send, phi_recv, part_send,
     part_recv, ready) = refs
    cell_out, panel_out = both.at[0], both.at[1]
    freqs, local = own_q.shape[0], own_q.shape[1]
    rows, share = 2 * freqs, local * 128
    z, x, c = lax.axis_index("blk"), lax.axis_index("cell"), lax.axis_index("col")
    hops = range(1, n_cell)

    def beside(dx):
        return lax.rem(x + dx, n_cell)

    def remote(src, dst, send, recv, zz, xx, cc):
        return pltpu.make_async_remote_copy(
            src_ref=src, dst_ref=dst, send_sem=send, recv_sem=recv,
            device_id={"blk": zz, "cell": xx, "col": cc}, device_id_type=MESH)

    def other_layers(step, nearest):
        def at(t, carry):
            dist = t if nearest else n_blk - t
            pl.when(z >= dist)(lambda: step(z - dist))
            pl.when(z + dist < n_blk)(lambda: step(z + dist))
            return carry

        lax.fori_loop(1, n_blk, at, 0)

    barrier = pltpu.get_barrier_semaphore()

    def greet(zz, xx, cc):
        pl.semaphore_signal(
            barrier, device_id={"blk": zz, "cell": xx, "col": cc}, device_id_type=MESH)

    def greet_layer(zz):
        greet(zz, x, 0)
        greet(zz, x, 1)

    def layers_below(step):
        def at(t, carry):
            step(t)
            return carry

        lax.fori_loop(0, z, at, 0)

    def layers_above(step):
        def at(t, carry):
            step(t)
            return carry

        lax.fori_loop(z + 1, n_blk, at, 0)

    for dx in range(n_cell):
        for dc in range(2):
            if dx or dc:
                greet(z, beside(dx), lax.rem(c + dc, 2))
    layers_above(greet_layer)

    def load(i, src, dst):
        return pltpu.make_async_copy(src, dst, load_sem.at[i])

    loads = [
        load(0, charges, own_q), load(1, currents, own_i), load(2, ends_hbm, ends),
        load(3, resist_hbm, resist), load(4, omegas_hbm, omegas), load(5, l_cols, b_cols),
    ]
    late_loads = [load(6, l_blocks, b_blocks), load(7, currents, b_arr.at[z, x])]
    core_loads = [
        load(8, p_cols, a_cols), load(9, p_blocks, a_blocks), load(10, charges, a_arr.at[z, x, 1])]

    pl.semaphore_wait(barrier, 2 * n_cell - 1 + 2 * z)

    def a_copy(zz, xx):
        return remote(charges, a_arr.at[z, x, c], a_send.at[zz, xx], a_recv.at[z, x, c], zz, xx, 1)

    def b_copy(zz, xx):
        return remote(currents, b_arr.at[z, x], b_send.at[zz, xx], b_recv.at[z, x], zz, xx, c)

    def answer(zz):
        def tell(cc):
            pl.semaphore_signal(
                ready.at[z], device_id={"blk": zz, "cell": x, "col": cc}, device_id_type=MESH)

        tell(0)
        pl.when(c == 1)(lambda: tell(1))

    layers_below(lambda zz: a_copy(zz, x).start())
    layers_below(answer)
    for dx in hops:
        a_copy(z, beside(dx)).start()
    pl.when(c == 0)(lambda: a_copy(z, x).start())
    layers_below(lambda zz: b_copy(zz, x).start())
    for dx in hops:
        b_copy(z, beside(dx)).start()
    for one in loads + late_loads:
        one.start()

    @pl.when(c == 1)
    def _():
        for one in core_loads:
            one.start()

    for one in loads:
        one.wait()

    def flat(ref):
        return jnp.concatenate(
            [ref[:, j].astype(jnp.float32).reshape(rows, 128) for j in range(local)], axis=1)

    i32 = flat(own_i)
    i16 = i32.astype(jnp.bfloat16)
    start = ends[0:1, :]
    stop = ends[1:2, :]
    chunk = 128
    base = lax.broadcasted_iota(jnp.int32, (chunk, share), 0)

    def fill(t, carry):
        offset = pl.multiple_of(t * chunk, chunk)
        plus = jnp.where(base == start - offset, 1.0, 0.0)
        minus = jnp.where(base == stop - offset, 1.0, 0.0)
        inc[pl.ds(offset, chunk), :] = (plus - minus).astype(jnp.bfloat16)
        return carry

    lax.fori_loop(0, n_cell * share // chunk, fill, 0)

    def inc_of(owner):
        return inc[pl.ds(pl.multiple_of(owner * share, share), share), :]

    def part_copy(dx):
        return remote(
            part_out.at[dx], part_in.at[dx], part_send.at[dx], part_recv.at[dx], z, beside(dx), c)

    for dx in hops:
        part_out[dx] = dot(i16, inc_of(beside(dx)), NT).astype(jnp.bfloat16)
        part_copy(dx).start()

    def send_up(zz):
        pl.semaphore_wait(ready.at[zz], 2 - c)
        a_copy(zz, x).start()
        b_copy(zz, x).start()

    layers_above(send_up)

    outflow = dot(i16, inc_of(x), NT)
    row = lax.broadcasted_iota(jnp.int32, (rows, 128), 0) // 2
    omega = jnp.zeros((rows, 128), jnp.float32)
    for f in range(freqs):
        omega = jnp.where(row == f, omegas[f], omega)
    omega = jnp.concatenate([omega] * local, axis=1)
    panel = outflow + omega * quarter_turn(flat(own_q))

    def a_piece(zz, xx, cc):
        return remote(
            charges, a_arr.at[zz, xx, cc], a_send.at[zz, xx], a_recv.at[zz, xx, cc], zz, xx, cc)

    def b_piece(zz, xx):
        return remote(currents, b_arr.at[zz, xx], b_send.at[zz, xx], b_recv.at[zz, xx], zz, xx, c)

    def a_forward(zz, dx, cc):
        piece = a_arr.at[zz, x, cc]
        return remote(piece, piece, a_pass.at[zz, dx, cc], a_recv.at[zz, x, cc], z, beside(dx), c)

    def b_forward(zz, dx):
        piece = b_arr.at[zz, x]
        return remote(piece, piece, b_pass.at[zz, dx], b_recv.at[zz, x], z, beside(dx), c)

    def products(zz, arr, mat, cols, blocks, acc, first):
        for xx in range(n_cell):
            for j in range(local):
                mat[zz, xx * local + j] = arr(xx, j)
        for r in range(local):
            left = jnp.concatenate([mat[zz, cols[r, k, zz]] for k in range(2)], axis=1)
            right = jnp.concatenate([blocks[r, zz, k] for k in range(2)], axis=1)
            term = dot(left, right, NT)
            if first:
                acc[r] = term
            else:
                acc[r] += term

    def a_products(zz, first):
        def arr(xx, j):
            return a_arr[zz, xx, :, :, j].reshape(2 * rows, 128)

        products(zz, arr, a_mat, a_cols, a_blocks, a_acc, first)

    def b_products(zz, first):
        def arr(xx, j):
            return b_arr[zz, xx, :, j].reshape(rows, 128)

        products(zz, arr, b_mat, b_cols, b_blocks, b_acc, first)

    def a_pass_on(zz):
        for cc in range(2):
            a_piece(zz, x, cc).wait_recv()
            for dx in hops:
                a_forward(zz, dx, cc).start()

    def b_pass_on(zz):
        b_piece(zz, x).wait_recv()
        for dx in hops:
            b_forward(zz, dx).start()

    def a_take(zz, first=False):
        for dx in hops:
            for cc in range(2):
                a_piece(zz, beside(dx), cc).wait_recv()
        a_products(zz, first)

    def b_take(zz, first=False):
        for dx in hops:
            b_piece(zz, beside(dx)).wait_recv()
        b_products(zz, first)

    def phi_copy(dx, cc):
        return remote(
            phi_out.at[cc], phi_in.at[x], phi_send.at[dx, cc], phi_recv.at[x], z, beside(dx), cc)

    def wait_phi(xx):
        remote(phi_out.at[0], phi_in.at[xx], phi_send.at[0, 0], phi_recv.at[xx], z, xx, c).wait_recv()

    @pl.when(c == 1)
    def _():
        other_layers(a_pass_on, True)
        for one in core_loads:
            one.wait()
        a_piece(z, x, 0).wait_recv()
        a_take(z, True)
        other_layers(b_pass_on, True)
        other_layers(a_take, True)
        phi = jnp.concatenate([a_acc[r] for r in range(local)], axis=1).astype(jnp.bfloat16)
        phi_out[0] = phi[:rows]
        for dx in hops:
            phi_copy(dx, 0).start()
        phi_out[1] = phi[rows:]
        for dx in hops:
            phi_copy(dx, 1).start()
        phi_copy(0, 0).start()
        phi_in[x] = phi[rows:]

    @pl.when(c == 0)
    def _():
        other_layers(b_pass_on, True)

    for one in late_loads:
        one.wait()
    b_take(z, True)
    other_layers(b_take, True)

    for dx in hops:
        part_copy(dx).wait_recv()
        panel += part_in[dx].astype(jnp.float32)
    panel_out[...] = panel.reshape(panel_out.shape)

    turned = quarter_turn(jnp.concatenate([b_acc[r] for r in range(local)], axis=1))
    cell = resist[...] * i32 + omega * turned
    pl.when(c == 0)(lambda: wait_phi(x))
    cell += dot(phi_in[x], inc_of(x), NN)
    for dx in hops:
        wait_phi(beside(dx))
        cell += dot(phi_in[beside(dx)], inc_of(beside(dx)), NN)
    cell_out[...] = cell.reshape(cell_out.shape)

    def sent(zz):
        a_copy(zz, x).wait_send()
        b_copy(zz, x).wait_send()
        for dx in hops:
            b_forward(zz, dx).wait_send()

            @pl.when(c == 1)
            def _(dx=dx):
                a_forward(zz, dx, 0).wait_send()
                a_forward(zz, dx, 1).wait_send()

    other_layers(sent, True)
    for dx in hops:
        part_copy(dx).wait_send()
        a_copy(z, beside(dx)).wait_send()
        b_copy(z, beside(dx)).wait_send()
    pl.when(c == 0)(lambda: a_copy(z, x).wait_send())

    @pl.when(c == 1)
    def _():
        phi_copy(0, 0).wait_send()
        for dx in hops:
            phi_copy(dx, 0).wait_send()
            phi_copy(dx, 1).wait_send()


def per_device(p_blocks, p_cols, l_blocks, l_cols, charges, currents, omegas, resist, branch_ends):
    n_blk, n_cell = lax.axis_size("blk"), lax.axis_size("cell")
    freqs, _, share = charges.shape
    rows, local = 2 * freqs, share // 128
    vmem, dma = pltpu.VMEM, pltpu.SemaphoreType.DMA

    def by_block(v):
        return v.reshape(freqs, 2, local, 128).transpose(0, 2, 1, 3)

    operands = (
        by_block(charges), by_block(currents), branch_ends, resist.reshape(1, share), omegas,
        p_cols.transpose(0, 2, 1), l_cols.transpose(0, 2, 1), p_blocks, l_blocks,
    )
    own = (freqs, local, 2, 128)
    bf16, f32 = jnp.bfloat16, jnp.float32
    outs = pl.pallas_call(
        functools.partial(kernel, n_blk, n_cell),
        out_shape=pltpu.VMEM((2, freqs, 2, share), f32),
        in_specs=[pl.BlockSpec(memory_space=pltpu.HBM)] * len(operands),
        out_specs=pl.BlockSpec(memory_space=vmem),
        scratch_shapes=[
            vmem((n_blk, n_cell, 2) + own, bf16),
            vmem((n_blk, n_cell) + own, bf16),
            vmem((n_blk, n_cell * local, 2 * rows, 128), bf16),
            vmem((n_blk, n_cell * local, rows, 128), bf16),
            vmem(own, bf16),
            vmem(own, bf16),
            vmem(branch_ends.shape, jnp.int32),
            vmem((1, share), f32),
            pltpu.SMEM(omegas.shape, f32),
            pltpu.SMEM((local, 2, n_blk), jnp.int32),
            pltpu.SMEM((local, 2, n_blk), jnp.int32),
            vmem(p_blocks.shape, bf16),
            vmem(l_blocks.shape, bf16),
            vmem((local, 2 * rows, 128), f32),
            vmem((local, rows, 128), f32),
            vmem((n_cell * share, share), bf16),
            vmem((2, rows, share), bf16),
            vmem((n_cell, rows, share), bf16),
            vmem((n_cell, rows, share), bf16),
            vmem((n_cell, rows, share), bf16),
            dma((11,)),
            dma((n_blk, n_cell)), dma((n_blk, n_cell, 2)), dma((n_blk, n_cell, 2)),
            dma((n_blk, n_cell)), dma((n_blk, n_cell)), dma((n_blk, n_cell)),
            dma((n_cell, 2)), dma((n_cell,)),
            dma((n_cell,)), dma((n_cell,)),
            pltpu.SemaphoreType.REGULAR((n_blk,)),
        ],
        compiler_params=pltpu.CompilerParams(
            collective_id=0, has_side_effects=True, vmem_limit_bytes=60 * 2**20
        ),
    )(*[pltpu.with_memory_space_constraint(v, pltpu.HBM) for v in operands])
    return outs[0], outs[1]


def solution(mesh):
    across = ("job", "blk", "cell")
    placed = (
        P(across, None, None, None, None),
        P(across, None, None),
        P(across, None, None, None, None),
        P(across, None, None),
        P("col", None, across),
        P("col", None, across),
        P("col"),
        P(across),
        P(None, across),
    )
    return jax.shard_map(
        per_device,
        mesh=mesh,
        in_specs=placed,
        out_specs=(P("col", None, across), P("col", None, across)),
        check_vma=False,
    )
```

```python
import functools

import jax
import jax.numpy as jnp
from jax import lax
from jax.experimental import pallas as pl
from jax.experimental.pallas import tpu as pltpu
from jax.sharding import PartitionSpec as P

MESH = pl.DeviceIdType.MESH
NT = (((1,), (1,)), ((), ()))
NN = (((1,), (0,)), ((), ()))


def dot(a, b, dims):
    return lax.dot_general(a, b, dims, preferred_element_type=jnp.float32)


def quarter_turn(x):
    rows = x.shape[0]
    even = lax.broadcasted_iota(jnp.int32, x.shape, 0) % 2 == 0
    return jnp.where(even, -pltpu.roll(x, rows - 1, 0), pltpu.roll(x, 1, 0))


def kernel(n_blk, n_cell, *refs):
    (charges, currents, ends_hbm, resist_hbm, omegas_hbm, p_cols, l_cols, p_blocks, l_blocks,
     both, a_arr, b_arr, a_mat, b_mat, own_q, own_i, ends, resist, omegas, a_cols, b_cols,
     a_blocks, b_blocks, a_acc, b_acc, inc, phi_out, phi_in, part_out, part_in, load_sem,
     a_send, a_recv, a_pass, b_send, b_recv, b_pass, phi_send, phi_recv, part_send,
     part_recv, ready, ready_beside) = refs
    cell_out, panel_out = both.at[0], both.at[1]
    freqs, local = own_q.shape[0], own_q.shape[1]
    rows, share = 2 * freqs, local * 128
    z, x, c = lax.axis_index("blk"), lax.axis_index("cell"), lax.axis_index("col")
    hops = range(1, n_cell)

    def beside(dx):
        return lax.rem(x + dx, n_cell)

    def remote(src, dst, send, recv, zz, xx, cc):
        return pltpu.make_async_remote_copy(
            src_ref=src, dst_ref=dst, send_sem=send, recv_sem=recv,
            device_id={"blk": zz, "cell": xx, "col": cc}, device_id_type=MESH)

    def other_layers(step, nearest):
        def at(t, carry):
            dist = t if nearest else n_blk - t
            pl.when(z >= dist)(lambda: step(z - dist))
            pl.when(z + dist < n_blk)(lambda: step(z + dist))
            return carry

        lax.fori_loop(1, n_blk, at, 0)

    barrier = pltpu.get_barrier_semaphore()

    def greet(zz, xx, cc):
        pl.semaphore_signal(
            barrier, device_id={"blk": zz, "cell": xx, "col": cc}, device_id_type=MESH)

    def loop(first, last, step):
        def at(t, carry):
            step(t)
            return carry

        lax.fori_loop(first, last, at, 0)

    def layers_below(step):
        loop(0, z, step)

    def layers_above(step):
        loop(z + 1, n_blk, step)

    def greet_chip(zz, xx):
        greet(zz, xx, 0)
        greet(zz, xx, 1)

    greet(z, x, 1 - c)
    loop(x + 1, n_cell, lambda xx: greet_chip(z, xx))
    layers_above(lambda zz: greet_chip(zz, x))

    def load(i, src, dst):
        return pltpu.make_async_copy(src, dst, load_sem.at[i])

    loads = [
        load(0, charges, own_q), load(1, currents, own_i), load(2, ends_hbm, ends),
        load(3, resist_hbm, resist), load(4, omegas_hbm, omegas), load(5, l_cols, b_cols),
    ]
    late_loads = [load(6, l_blocks, b_blocks), load(7, currents, b_arr.at[z, x])]
    core_loads = [
        load(8, p_cols, a_cols), load(9, p_blocks, a_blocks), load(10, charges, a_arr.at[z, x, 1])]

    pl.semaphore_wait(barrier, 1 + 2 * (x + z))

    def a_copy(zz, xx):
        return remote(charges, a_arr.at[z, x, c], a_send.at[zz, xx], a_recv.at[z, x, c], zz, xx, 1)

    def b_copy(zz, xx):
        return remote(currents, b_arr.at[z, x], b_send.at[zz, xx], b_recv.at[z, x], zz, xx, c)

    def answer(zz):
        def tell(cc):
            pl.semaphore_signal(
                ready.at[z], device_id={"blk": zz, "cell": x, "col": cc}, device_id_type=MESH)

        tell(0)
        pl.when(c == 1)(lambda: tell(1))

    def answer_beside(xx):
        for cc in range(2):
            pl.semaphore_signal(
                ready_beside.at[x], device_id={"blk": z, "cell": xx, "col": cc}, device_id_type=MESH)

    def send(zz, xx):
        a_copy(zz, xx).start()
        b_copy(zz, xx).start()

    layers_below(answer)
    layers_below(lambda zz: send(zz, x))
    loop(0, x, answer_beside)
    loop(0, x, lambda xx: send(z, xx))
    pl.when(c == 0)(lambda: a_copy(z, x).start())
    for one in loads + late_loads:
        one.start()

    @pl.when(c == 1)
    def _():
        for one in core_loads:
            one.start()

    for one in loads:
        one.wait()

    def send_beside(xx):
        pl.semaphore_wait(ready_beside.at[xx], 2)
        send(z, xx)

    loop(x + 1, n_cell, send_beside)

    def flat(ref):
        return jnp.concatenate(
            [ref[:, j].astype(jnp.float32).reshape(rows, 128) for j in range(local)], axis=1)

    i32 = flat(own_i)
    i16 = i32.astype(jnp.bfloat16)
    start = ends[0:1, :]
    stop = ends[1:2, :]
    chunk = 128
    base = lax.broadcasted_iota(jnp.int32, (chunk, share), 0)

    def fill(t, carry):
        offset = pl.multiple_of(t * chunk, chunk)
        plus = jnp.where(base == start - offset, 1.0, 0.0)
        minus = jnp.where(base == stop - offset, 1.0, 0.0)
        inc[pl.ds(offset, chunk), :] = (plus - minus).astype(jnp.bfloat16)
        return carry

    lax.fori_loop(0, n_cell * share // chunk, fill, 0)

    def inc_of(owner):
        return inc[pl.ds(pl.multiple_of(owner * share, share), share), :]

    def part_copy(dx):
        return remote(
            part_out.at[dx], part_in.at[dx], part_send.at[dx], part_recv.at[dx], z, beside(dx), c)

    for dx in hops:
        part_out[dx] = dot(i16, inc_of(beside(dx)), NT).astype(jnp.bfloat16)
        part_copy(dx).start()

    def send_up(zz):
        pl.semaphore_wait(ready.at[zz], 2 - c)
        send(zz, x)

    layers_above(send_up)

    outflow = dot(i16, inc_of(x), NT)
    row = lax.broadcasted_iota(jnp.int32, (rows, 128), 0) // 2
    omega = jnp.zeros((rows, 128), jnp.float32)
    for f in range(freqs):
        omega = jnp.where(row == f, omegas[f], omega)
    omega = jnp.concatenate([omega] * local, axis=1)
    panel = outflow + omega * quarter_turn(flat(own_q))

    def a_piece(zz, xx, cc):
        return remote(
            charges, a_arr.at[zz, xx, cc], a_send.at[zz, xx], a_recv.at[zz, xx, cc], zz, xx, cc)

    def b_piece(zz, xx):
        return remote(currents, b_arr.at[zz, xx], b_send.at[zz, xx], b_recv.at[zz, xx], zz, xx, c)

    def a_forward(zz, dx, cc):
        piece = a_arr.at[zz, x, cc]
        return remote(piece, piece, a_pass.at[zz, dx, cc], a_recv.at[zz, x, cc], z, beside(dx), c)

    def b_forward(zz, dx):
        piece = b_arr.at[zz, x]
        return remote(piece, piece, b_pass.at[zz, dx], b_recv.at[zz, x], z, beside(dx), c)

    def products(zz, arr, mat, cols, blocks, acc, first):
        for xx in range(n_cell):
            for j in range(local):
                mat[zz, xx * local + j] = arr(xx, j)
        for r in range(local):
            left = jnp.concatenate([mat[zz, cols[r, k, zz]] for k in range(2)], axis=1)
            right = jnp.concatenate([blocks[r, zz, k] for k in range(2)], axis=1)
            term = dot(left, right, NT)
            if first:
                acc[r] = term
            else:
                acc[r] += term

    def a_products(zz, first):
        def arr(xx, j):
            return a_arr[zz, xx, :, :, j].reshape(2 * rows, 128)

        products(zz, arr, a_mat, a_cols, a_blocks, a_acc, first)

    def b_products(zz, first):
        def arr(xx, j):
            return b_arr[zz, xx, :, j].reshape(rows, 128)

        products(zz, arr, b_mat, b_cols, b_blocks, b_acc, first)

    def a_pass_on(zz):
        for cc in (1, 0):
            a_piece(zz, x, cc).wait_recv()
            for dx in hops:
                a_forward(zz, dx, cc).start()

    def b_pass_on(zz):
        b_piece(zz, x).wait_recv()
        for dx in hops:
            b_forward(zz, dx).start()

    def a_take(zz, first=False):
        for dx in hops:
            for cc in range(2):
                a_piece(zz, beside(dx), cc).wait_recv()
        a_products(zz, first)

    def b_take(zz, first=False):
        for dx in hops:
            b_piece(zz, beside(dx)).wait_recv()
        b_products(zz, first)

    def phi_copy(dx, cc):
        return remote(
            phi_out.at[cc], phi_in.at[x], phi_send.at[dx, cc], phi_recv.at[x], z, beside(dx), cc)

    def wait_phi(xx):
        remote(phi_out.at[0], phi_in.at[xx], phi_send.at[0, 0], phi_recv.at[xx], z, xx, c).wait_recv()

    @pl.when(c == 1)
    def _():
        other_layers(a_pass_on, True)
        for one in core_loads:
            one.wait()
        a_piece(z, x, 0).wait_recv()
        a_take(z, True)
        other_layers(b_pass_on, True)
        other_layers(a_take, True)
        phi = jnp.concatenate([a_acc[r] for r in range(local)], axis=1).astype(jnp.bfloat16)
        phi_out[0] = phi[:rows]
        for dx in hops:
            phi_copy(dx, 0).start()
        phi_out[1] = phi[rows:]
        for dx in hops:
            phi_copy(dx, 1).start()
        phi_copy(0, 0).start()
        phi_in[x] = phi[rows:]

    @pl.when(c == 0)
    def _():
        other_layers(b_pass_on, True)

    for one in late_loads:
        one.wait()
    b_take(z, True)
    other_layers(b_take, True)

    for dx in hops:
        part_copy(dx).wait_recv()
        panel += part_in[dx].astype(jnp.float32)
    panel_out[...] = panel.reshape(panel_out.shape)

    turned = quarter_turn(jnp.concatenate([b_acc[r] for r in range(local)], axis=1))
    cell = resist[...] * i32 + omega * turned
    pl.when(c == 0)(lambda: wait_phi(x))
    cell += dot(phi_in[x], inc_of(x), NN)
    for dx in hops:
        wait_phi(beside(dx))
        cell += dot(phi_in[beside(dx)], inc_of(beside(dx)), NN)
    cell_out[...] = cell.reshape(cell_out.shape)

    def sent(zz):
        a_copy(zz, x).wait_send()
        b_copy(zz, x).wait_send()
        for dx in hops:
            b_forward(zz, dx).wait_send()

            @pl.when(c == 1)
            def _(dx=dx):
                a_forward(zz, dx, 0).wait_send()
                a_forward(zz, dx, 1).wait_send()

    other_layers(sent, True)
    for dx in hops:
        part_copy(dx).wait_send()
        a_copy(z, beside(dx)).wait_send()
        b_copy(z, beside(dx)).wait_send()
    pl.when(c == 0)(lambda: a_copy(z, x).wait_send())

    @pl.when(c == 1)
    def _():
        phi_copy(0, 0).wait_send()
        for dx in hops:
            phi_copy(dx, 0).wait_send()
            phi_copy(dx, 1).wait_send()


def per_device(p_blocks, p_cols, l_blocks, l_cols, charges, currents, omegas, resist, branch_ends):
    n_blk, n_cell = lax.axis_size("blk"), lax.axis_size("cell")
    freqs, _, share = charges.shape
    rows, local = 2 * freqs, share // 128
    vmem, dma = pltpu.VMEM, pltpu.SemaphoreType.DMA

    def by_block(v):
        return v.reshape(freqs, 2, local, 128).transpose(0, 2, 1, 3)

    operands = (
        by_block(charges), by_block(currents), branch_ends, resist.reshape(1, share), omegas,
        p_cols.transpose(0, 2, 1), l_cols.transpose(0, 2, 1), p_blocks, l_blocks,
    )
    own = (freqs, local, 2, 128)
    bf16, f32 = jnp.bfloat16, jnp.float32
    outs = pl.pallas_call(
        functools.partial(kernel, n_blk, n_cell),
        out_shape=pltpu.VMEM((2, freqs, 2, share), f32),
        in_specs=[pl.BlockSpec(memory_space=pltpu.HBM)] * len(operands),
        out_specs=pl.BlockSpec(memory_space=vmem),
        scratch_shapes=[
            vmem((n_blk, n_cell, 2) + own, bf16),
            vmem((n_blk, n_cell) + own, bf16),
            vmem((n_blk, n_cell * local, 2 * rows, 128), bf16),
            vmem((n_blk, n_cell * local, rows, 128), bf16),
            vmem(own, bf16),
            vmem(own, bf16),
            vmem(branch_ends.shape, jnp.int32),
            vmem((1, share), f32),
            pltpu.SMEM(omegas.shape, f32),
            pltpu.SMEM((local, 2, n_blk), jnp.int32),
            pltpu.SMEM((local, 2, n_blk), jnp.int32),
            vmem(p_blocks.shape, bf16),
            vmem(l_blocks.shape, bf16),
            vmem((local, 2 * rows, 128), f32),
            vmem((local, rows, 128), f32),
            vmem((n_cell * share, share), bf16),
            vmem((2, rows, share), bf16),
            vmem((n_cell, rows, share), bf16),
            vmem((n_cell, rows, share), bf16),
            vmem((n_cell, rows, share), bf16),
            dma((11,)),
            dma((n_blk, n_cell)), dma((n_blk, n_cell, 2)), dma((n_blk, n_cell, 2)),
            dma((n_blk, n_cell)), dma((n_blk, n_cell)), dma((n_blk, n_cell)),
            dma((n_cell, 2)), dma((n_cell,)),
            dma((n_cell,)), dma((n_cell,)),
            pltpu.SemaphoreType.REGULAR((n_blk,)),
            pltpu.SemaphoreType.REGULAR((n_cell,)),
        ],
        compiler_params=pltpu.CompilerParams(
            collective_id=0, has_side_effects=True, vmem_limit_bytes=60 * 2**20
        ),
    )(*[pltpu.with_memory_space_constraint(v, pltpu.HBM) for v in operands])
    return outs[0], outs[1]


def solution(mesh):
    across = ("job", "blk", "cell")
    placed = (
        P(across, None, None, None, None),
        P(across, None, None),
        P(across, None, None, None, None),
        P(across, None, None),
        P("col", None, across),
        P("col", None, across),
        P("col"),
        P(across),
        P(None, across),
    )
    return jax.shard_map(
        per_device,
        mesh=mesh,
        in_specs=placed,
        out_specs=(P("col", None, across), P("col", None, across)),
        check_vma=False,
    )
```

```python
import functools

import jax
import jax.numpy as jnp
from jax import lax
from jax.experimental import pallas as pl
from jax.experimental.pallas import tpu as pltpu
from jax.sharding import PartitionSpec as P

MESH = pl.DeviceIdType.MESH
NT = (((1,), (1,)), ((), ()))
NN = (((1,), (0,)), ((), ()))


def dot(a, b, dims):
    return lax.dot_general(a, b, dims, preferred_element_type=jnp.float32)


def quarter_turn(x):
    rows = x.shape[0]
    even = lax.broadcasted_iota(jnp.int32, x.shape, 0) % 2 == 0
    return jnp.where(even, -pltpu.roll(x, rows - 1, 0), pltpu.roll(x, 1, 0))


def kernel(n_blk, n_cell, *refs):
    (charges, currents, ends_hbm, resist_hbm, omegas_hbm, p_cols, l_cols, p_blocks, l_blocks,
     both, a_arr, b_arr, a_mat, b_mat, own_q, own_i, ends, resist, omegas, a_cols, b_cols,
     a_blocks, b_blocks, a_acc, b_acc, inc, phi_out, phi_in, part_out, part_in, load_sem,
     a_send, a_recv, a_pass, b_send, b_recv, b_pass, phi_send, phi_recv, part_send,
     part_recv, ready, ready_beside) = refs
    cell_out, panel_out = both.at[0], both.at[1]
    freqs, local = own_q.shape[0], own_q.shape[1]
    rows, share = 2 * freqs, local * 128
    z, x, c = lax.axis_index("blk"), lax.axis_index("cell"), lax.axis_index("col")
    hops = range(1, n_cell)

    def beside(dx):
        return lax.rem(x + dx, n_cell)

    def remote(src, dst, send, recv, zz, xx, cc):
        return pltpu.make_async_remote_copy(
            src_ref=src, dst_ref=dst, send_sem=send, recv_sem=recv,
            device_id={"blk": zz, "cell": xx, "col": cc}, device_id_type=MESH)

    def other_layers(step, nearest):
        def at(t, carry):
            dist = t if nearest else n_blk - t
            pl.when(z >= dist)(lambda: step(z - dist))
            pl.when(z + dist < n_blk)(lambda: step(z + dist))
            return carry

        lax.fori_loop(1, n_blk, at, 0)

    barrier = pltpu.get_barrier_semaphore()

    def greet(zz, xx, cc):
        pl.semaphore_signal(
            barrier, device_id={"blk": zz, "cell": xx, "col": cc}, device_id_type=MESH)

    def loop(first, last, step):
        def at(t, carry):
            step(t)
            return carry

        lax.fori_loop(first, last, at, 0)

    def layers_below(step):
        loop(0, z, step)

    def layers_above(step):
        loop(z + 1, n_blk, step)

    def greet_chip(zz, xx):
        greet(zz, xx, 0)
        greet(zz, xx, 1)

    greet(z, x, 1 - c)
    loop(x + 1, n_cell, lambda xx: greet_chip(z, xx))
    layers_above(lambda zz: greet_chip(zz, x))

    def first_last(zz):
        return (zz == n_blk - 1) & (z == 0) & (c == 0) & (n_blk > 1)

    last_first = (z == n_blk - 1) & (c == 0) & (n_blk > 1)

    @pl.when((z == 0) & (c == 0) & (n_blk > 1))
    def _():
        for dx in hops:
            greet(n_blk - 1, beside(dx), 0)


    def load(i, src, dst):
        return pltpu.make_async_copy(src, dst, load_sem.at[i])

    loads = [
        load(0, charges, own_q), load(1, currents, own_i), load(2, ends_hbm, ends),
        load(3, resist_hbm, resist), load(4, omegas_hbm, omegas), load(5, l_cols, b_cols),
    ]
    late_loads = [load(6, l_blocks, b_blocks), load(7, currents, b_arr.at[z, x])]
    core_loads = [
        load(8, p_cols, a_cols), load(9, p_blocks, a_blocks), load(10, charges, a_arr.at[z, x, 1])]

    pl.semaphore_wait(barrier, 1 + 2 * (x + z) + jnp.where(last_first, n_cell - 1, 0))

    def a_copy(zz, xx):
        return remote(charges, a_arr.at[z, x, c], a_send.at[zz, xx], a_recv.at[z, x, c], zz, xx, 1)

    def b_copy(zz, xx):
        return remote(currents, b_arr.at[z, x], b_send.at[zz, xx], b_recv.at[z, x], zz, xx, c)

    def answer(zz):
        def tell(cc):
            pl.semaphore_signal(
                ready.at[z], device_id={"blk": zz, "cell": x, "col": cc}, device_id_type=MESH)

        tell(0)
        pl.when(c == 1)(lambda: tell(1))

    def answer_beside(xx):
        for cc in range(2):
            pl.semaphore_signal(
                ready_beside.at[x], device_id={"blk": z, "cell": xx, "col": cc}, device_id_type=MESH)

    def send(zz, xx):
        a_copy(zz, xx).start()
        b_copy(zz, xx).start()

    layers_below(answer)
    pl.when(z > 0)(lambda: send(0, x))

    @pl.when(last_first)
    def _():
        for dx in hops:
            b_copy(0, beside(dx)).start()

    loop(0, x, answer_beside)
    loop(0, x, lambda xx: send(z, xx))
    pl.when(c == 0)(lambda: a_copy(z, x).start())

    for one in loads + late_loads:
        one.start()

    @pl.when(c == 1)
    def _():
        for one in core_loads:
            one.start()

    for one in loads:
        one.wait()

    def flat(ref):
        return jnp.concatenate(
            [ref[:, j].astype(jnp.float32).reshape(rows, 128) for j in range(local)], axis=1)

    i32 = flat(own_i)
    i16 = i32.astype(jnp.bfloat16)
    start = ends[0:1, :]
    stop = ends[1:2, :]
    chunk = 128
    base = lax.broadcasted_iota(jnp.int32, (chunk, share), 0)

    def fill(t, carry):
        offset = pl.multiple_of(t * chunk, chunk)
        plus = jnp.where(base == start - offset, 1.0, 0.0)
        minus = jnp.where(base == stop - offset, 1.0, 0.0)
        inc[pl.ds(offset, chunk), :] = (plus - minus).astype(jnp.bfloat16)
        return carry

    lax.fori_loop(0, n_cell * share // chunk, fill, 0)

    loop(1, z, lambda zz: send(zz, x))

    def inc_of(owner):
        return inc[pl.ds(pl.multiple_of(owner * share, share), share), :]

    def send_beside(xx):
        pl.semaphore_wait(ready_beside.at[xx], 2)
        send(z, xx)

    loop(x + 1, n_cell, send_beside)

    def part_copy(dx):
        return remote(
            part_out.at[dx], part_in.at[dx], part_send.at[dx], part_recv.at[dx], z, beside(dx), c)

    for dx in hops:
        part_out[dx] = dot(i16, inc_of(beside(dx)), NT).astype(jnp.bfloat16)
        part_copy(dx).start()

    def send_up(zz):
        pl.semaphore_wait(ready.at[zz], 2 - c)
        send(zz, x)

    layers_above(send_up)

    outflow = dot(i16, inc_of(x), NT)
    row = lax.broadcasted_iota(jnp.int32, (rows, 128), 0) // 2
    omega = jnp.zeros((rows, 128), jnp.float32)
    for f in range(freqs):
        omega = jnp.where(row == f, omegas[f], omega)
    omega = jnp.concatenate([omega] * local, axis=1)
    panel = outflow + omega * quarter_turn(flat(own_q))

    def a_piece(zz, xx, cc):
        return remote(
            charges, a_arr.at[zz, xx, cc], a_send.at[zz, xx], a_recv.at[zz, xx, cc], zz, xx, cc)

    def b_piece(zz, xx):
        return remote(currents, b_arr.at[zz, xx], b_send.at[zz, xx], b_recv.at[zz, xx], zz, xx, c)

    def a_forward(zz, dx, cc):
        piece = a_arr.at[zz, x, cc]
        return remote(piece, piece, a_pass.at[zz, dx, cc], a_recv.at[zz, x, cc], z, beside(dx), c)

    def b_forward(zz, dx):
        piece = b_arr.at[zz, x]
        return remote(piece, piece, b_pass.at[zz, dx], b_recv.at[zz, x], z, beside(dx), c)

    def products(zz, arr, mat, cols, blocks, acc, first):
        for xx in range(n_cell):
            for j in range(local):
                mat[zz, xx * local + j] = arr(xx, j)
        for r in range(local):
            left = jnp.concatenate([mat[zz, cols[r, k, zz]] for k in range(2)], axis=1)
            right = jnp.concatenate([blocks[r, zz, k] for k in range(2)], axis=1)
            term = dot(left, right, NT)
            if first:
                acc[r] = term
            else:
                acc[r] += term

    def a_products(zz, first):
        def arr(xx, j):
            return a_arr[zz, xx, :, :, j].reshape(2 * rows, 128)

        products(zz, arr, a_mat, a_cols, a_blocks, a_acc, first)

    def b_products(zz, first):
        def arr(xx, j):
            return b_arr[zz, xx, :, j].reshape(rows, 128)

        products(zz, arr, b_mat, b_cols, b_blocks, b_acc, first)

    def a_pass_on(zz):
        for cc in (1, 0):
            a_piece(zz, x, cc).wait_recv()
            for dx in hops:
                a_forward(zz, dx, cc).start()

    def b_pass_on(zz):
        b_piece(zz, x).wait_recv()

        @pl.when(jnp.logical_not(first_last(zz)))
        def _():
            for dx in hops:
                b_forward(zz, dx).start()

    def a_take(zz, first=False):
        for dx in hops:
            for cc in range(2):
                a_piece(zz, beside(dx), cc).wait_recv()
        a_products(zz, first)

    def b_take(zz, first=False):
        for dx in hops:
            b_piece(zz, beside(dx)).wait_recv()
        b_products(zz, first)

    def phi_copy(dx, cc):
        return remote(
            phi_out.at[cc], phi_in.at[x], phi_send.at[dx, cc], phi_recv.at[x], z, beside(dx), cc)

    def wait_phi(xx):
        remote(phi_out.at[0], phi_in.at[xx], phi_send.at[0, 0], phi_recv.at[xx], z, xx, c).wait_recv()

    @pl.when(c == 1)
    def _():
        other_layers(a_pass_on, True)
        for one in core_loads:
            one.wait()
        a_piece(z, x, 0).wait_recv()
        a_take(z, True)
        other_layers(b_pass_on, True)
        other_layers(a_take, True)
        phi = jnp.concatenate([a_acc[r] for r in range(local)], axis=1).astype(jnp.bfloat16)
        phi_out[0] = phi[:rows]
        for dx in hops:
            phi_copy(dx, 0).start()
        phi_out[1] = phi[rows:]
        for dx in hops:
            phi_copy(dx, 1).start()
        phi_copy(0, 0).start()
        phi_in[x] = phi[rows:]

    @pl.when(c == 0)
    def _():
        other_layers(b_pass_on, True)

    for one in late_loads:
        one.wait()
    b_take(z, True)
    other_layers(b_take, True)

    for dx in hops:
        part_copy(dx).wait_recv()
        panel += part_in[dx].astype(jnp.float32)
    panel_out[...] = panel.reshape(panel_out.shape)

    turned = quarter_turn(jnp.concatenate([b_acc[r] for r in range(local)], axis=1))
    cell = resist[...] * i32 + omega * turned
    pl.when(c == 0)(lambda: wait_phi(x))
    cell += dot(phi_in[x], inc_of(x), NN)
    for dx in hops:
        wait_phi(beside(dx))
        cell += dot(phi_in[beside(dx)], inc_of(beside(dx)), NN)
    cell_out[...] = cell.reshape(cell_out.shape)

    def sent(zz):
        a_copy(zz, x).wait_send()
        b_copy(zz, x).wait_send()
        for dx in hops:
            pl.when(jnp.logical_not(first_last(zz)))(lambda dx=dx: b_forward(zz, dx).wait_send())

            @pl.when(c == 1)
            def _(dx=dx):
                a_forward(zz, dx, 0).wait_send()
                a_forward(zz, dx, 1).wait_send()

    other_layers(sent, True)

    @pl.when(last_first)
    def _():
        for dx in hops:
            b_copy(0, beside(dx)).wait_send()

    for dx in hops:
        part_copy(dx).wait_send()
        a_copy(z, beside(dx)).wait_send()
        b_copy(z, beside(dx)).wait_send()
    pl.when(c == 0)(lambda: a_copy(z, x).wait_send())

    @pl.when(c == 1)
    def _():
        phi_copy(0, 0).wait_send()
        for dx in hops:
            phi_copy(dx, 0).wait_send()
            phi_copy(dx, 1).wait_send()


def per_device(p_blocks, p_cols, l_blocks, l_cols, charges, currents, omegas, resist, branch_ends):
    n_blk, n_cell = lax.axis_size("blk"), lax.axis_size("cell")
    freqs, _, share = charges.shape
    rows, local = 2 * freqs, share // 128
    vmem, dma = pltpu.VMEM, pltpu.SemaphoreType.DMA

    def by_block(v):
        return v.reshape(freqs, 2, local, 128).transpose(0, 2, 1, 3)

    operands = (
        by_block(charges), by_block(currents), branch_ends, resist.reshape(1, share), omegas,
        p_cols.transpose(0, 2, 1), l_cols.transpose(0, 2, 1), p_blocks, l_blocks,
    )
    own = (freqs, local, 2, 128)
    bf16, f32 = jnp.bfloat16, jnp.float32
    outs = pl.pallas_call(
        functools.partial(kernel, n_blk, n_cell),
        out_shape=pltpu.VMEM((2, freqs, 2, share), f32),
        in_specs=[pl.BlockSpec(memory_space=pltpu.HBM)] * len(operands),
        out_specs=pl.BlockSpec(memory_space=vmem),
        scratch_shapes=[
            vmem((n_blk, n_cell, 2) + own, bf16),
            vmem((n_blk, n_cell) + own, bf16),
            vmem((n_blk, n_cell * local, 2 * rows, 128), bf16),
            vmem((n_blk, n_cell * local, rows, 128), bf16),
            vmem(own, bf16),
            vmem(own, bf16),
            vmem(branch_ends.shape, jnp.int32),
            vmem((1, share), f32),
            pltpu.SMEM(omegas.shape, f32),
            pltpu.SMEM((local, 2, n_blk), jnp.int32),
            pltpu.SMEM((local, 2, n_blk), jnp.int32),
            vmem(p_blocks.shape, bf16),
            vmem(l_blocks.shape, bf16),
            vmem((local, 2 * rows, 128), f32),
            vmem((local, rows, 128), f32),
            vmem((n_cell * share, share), bf16),
            vmem((2, rows, share), bf16),
            vmem((n_cell, rows, share), bf16),
            vmem((n_cell, rows, share), bf16),
            vmem((n_cell, rows, share), bf16),
            dma((11,)),
            dma((n_blk, n_cell)), dma((n_blk, n_cell, 2)), dma((n_blk, n_cell, 2)),
            dma((n_blk, n_cell)), dma((n_blk, n_cell)), dma((n_blk, n_cell)),
            dma((n_cell, 2)), dma((n_cell,)),
            dma((n_cell,)), dma((n_cell,)),
            pltpu.SemaphoreType.REGULAR((n_blk,)),
            pltpu.SemaphoreType.REGULAR((n_cell,)),
        ],
        compiler_params=pltpu.CompilerParams(
            collective_id=0, has_side_effects=True, vmem_limit_bytes=60 * 2**20
        ),
    )(*[pltpu.with_memory_space_constraint(v, pltpu.HBM) for v in operands])
    return outs[0], outs[1]


def solution(mesh):
    across = ("job", "blk", "cell")
    placed = (
        P(across, None, None, None, None),
        P(across, None, None),
        P(across, None, None, None, None),
        P(across, None, None),
        P("col", None, across),
        P("col", None, across),
        P("col"),
        P(across),
        P(None, across),
    )
    return jax.shard_map(
        per_device,
        mesh=mesh,
        in_specs=placed,
        out_specs=(P("col", None, across), P("col", None, across)),
        check_vma=False,
    )
```

```python
import functools

import jax
import jax.numpy as jnp
from jax import lax
from jax.experimental import pallas as pl
from jax.experimental.pallas import tpu as pltpu
from jax.sharding import PartitionSpec as P

MESH = pl.DeviceIdType.MESH
NT = (((1,), (1,)), ((), ()))
NN = (((1,), (0,)), ((), ()))


def dot(a, b, dims):
    return lax.dot_general(a, b, dims, preferred_element_type=jnp.float32)


def quarter_turn(x):
    rows = x.shape[0]
    even = lax.broadcasted_iota(jnp.int32, x.shape, 0) % 2 == 0
    return jnp.where(even, -pltpu.roll(x, rows - 1, 0), pltpu.roll(x, 1, 0))


def kernel(n_blk, n_cell, *refs):
    (charges, currents, ends_hbm, resist_hbm, omegas_hbm, p_cols, l_cols, p_blocks, l_blocks,
     both, a_arr, b_arr, a_mat, b_mat, ends, resist, omegas, a_cols, b_cols,
     a_blocks, b_blocks, a_acc, b_acc, inc, phi_out, phi_in, part_out, part_in, load_sem,
     a_recv, a_side, b_recv, sent_sem, phi_recv, part_recv, ready, ready_beside) = refs
    cell_out, panel_out = both.at[0], both.at[1]
    freqs, local = charges.shape[0], charges.shape[1]
    rows, share = 2 * freqs, local * 128
    z, x, c = lax.axis_index("blk"), lax.axis_index("cell"), lax.axis_index("col")
    hops = range(1, n_cell)

    def beside(dx):
        return lax.rem(x + dx, n_cell)

    def remote(src, dst, send, recv, zz, xx, cc):
        return pltpu.make_async_remote_copy(
            src_ref=src, dst_ref=dst, send_sem=send, recv_sem=recv,
            device_id={"blk": zz, "cell": xx, "col": cc}, device_id_type=MESH)

    def other_layers(step, nearest):
        def at(t, carry):
            dist = t if nearest else n_blk - t
            pl.when(z >= dist)(lambda: step(z - dist))
            pl.when(z + dist < n_blk)(lambda: step(z + dist))
            return carry

        lax.fori_loop(1, n_blk, at, 0)

    barrier = pltpu.get_barrier_semaphore()

    def greet(zz, xx, cc):
        pl.semaphore_signal(
            barrier, device_id={"blk": zz, "cell": xx, "col": cc}, device_id_type=MESH)

    def loop(first, last, step):
        def at(t, carry):
            step(t)
            return carry

        lax.fori_loop(first, last, at, 0)

    def layers_below(step):
        loop(0, z, step)

    def layers_above(step):
        loop(z + 1, n_blk, step)

    def greet_chip(zz, xx):
        greet(zz, xx, 0)
        greet(zz, xx, 1)

    greet(z, x, 1 - c)
    loop(x + 1, n_cell, lambda xx: greet_chip(z, xx))
    layers_above(lambda zz: greet_chip(zz, x))

    def first_last(zz):
        return (zz == n_blk - 1) & (z == 0) & (c == 0) & (n_blk > 1)

    last_first = (z == n_blk - 1) & (c == 0) & (n_blk > 1)

    @pl.when((z == 0) & (c == 0) & (n_blk > 1))
    def _():
        for dx in hops:
            greet(n_blk - 1, beside(dx), 0)


    def load(i, src, dst):
        return pltpu.make_async_copy(src, dst, load_sem.at[i])

    loads = [
        load(0, charges, a_arr.at[z, x, c]), load(8, currents, b_arr.at[z, x]),
        load(1, ends_hbm, ends), load(2, resist_hbm, resist), load(3, omegas_hbm, omegas),
        load(4, l_cols, b_cols),
    ]
    late_loads = [load(5, l_blocks, b_blocks)]
    core_loads = [load(6, p_cols, a_cols), load(7, p_blocks, a_blocks)]

    pl.semaphore_wait(barrier, 1 + 2 * (x + z) + jnp.where(last_first, n_cell - 1, 0))

    def a_copy(zz, xx, on):
        arrives = a_side.at[z] if on == 1 else a_recv.at[z, c]
        return remote(charges, a_arr.at[z, x, c], sent_sem.at[on], arrives, zz, xx, 1)

    def b_copy(zz, xx, on):
        return remote(
            currents, b_arr.at[z, x], sent_sem.at[on], b_recv.at[z, min(on, 1)], zz, xx, c)

    def answer(zz):
        def tell(cc):
            pl.semaphore_signal(
                ready.at[z], device_id={"blk": zz, "cell": x, "col": cc}, device_id_type=MESH)

        tell(0)
        pl.when(c == 1)(lambda: tell(1))

    def answer_beside(xx):
        for cc in range(2):
            pl.semaphore_signal(
                ready_beside.at[x], device_id={"blk": z, "cell": xx, "col": cc}, device_id_type=MESH)

    def send(zz, xx, on):
        a_copy(zz, xx, on).start()
        b_copy(zz, xx, on).start()

    layers_below(answer)
    pl.when(z > 0)(lambda: send(0, x, 0))

    @pl.when(last_first)
    def _():
        for dx in hops:
            b_copy(0, beside(dx), 2).start()

    loop(0, x, answer_beside)
    loop(0, x, lambda xx: send(z, xx, 1))
    pl.when(c == 0)(lambda: a_copy(z, x, 2).start())

    for one in loads + late_loads:
        one.start()

    @pl.when(c == 1)
    def _():
        for one in core_loads:
            one.start()

    for one in loads:
        one.wait()

    def flat(ref):
        return jnp.concatenate(
            [ref[:, j].astype(jnp.float32).reshape(rows, 128) for j in range(local)], axis=1)

    i32 = flat(b_arr.at[z, x])
    i16 = i32.astype(jnp.bfloat16)
    start = ends[0:1, :]
    stop = ends[1:2, :]
    chunk = 128
    base = lax.broadcasted_iota(jnp.int32, (chunk, share), 0)

    def fill(t, carry):
        offset = pl.multiple_of(t * chunk, chunk)
        plus = jnp.where(base == start - offset, 1.0, 0.0)
        minus = jnp.where(base == stop - offset, 1.0, 0.0)
        inc[pl.ds(offset, chunk), :] = (plus - minus).astype(jnp.bfloat16)
        return carry

    lax.fori_loop(0, n_cell * share // chunk, fill, 0)

    loop(1, z, lambda zz: send(zz, x, 0))

    def inc_of(owner):
        return inc[pl.ds(pl.multiple_of(owner * share, share), share), :]

    def send_beside(xx):
        pl.semaphore_wait(ready_beside.at[xx], 2)
        send(z, xx, 1)

    loop(x + 1, n_cell, send_beside)

    def part_copy(dx):
        return remote(
            part_out.at[dx], part_in.at[dx], sent_sem.at[6], part_recv, z, beside(dx), c)

    for dx in hops:
        part_out[dx] = dot(i16, inc_of(beside(dx)), NT).astype(jnp.bfloat16)
        part_copy(dx).start()

    def send_up(zz):
        pl.semaphore_wait(ready.at[zz], 2 - c)
        send(zz, x, 0)

    layers_above(send_up)

    outflow = dot(i16, inc_of(x), NT)
    row = lax.broadcasted_iota(jnp.int32, (rows, 128), 0) // 2
    omega = jnp.zeros((rows, 128), jnp.float32)
    for f in range(freqs):
        omega = jnp.where(row == f, omegas[f], omega)
    omega = jnp.concatenate([omega] * local, axis=1)
    panel = outflow + omega * quarter_turn(flat(a_arr.at[z, x, c]))

    def landed(dst, sem):
        remote(dst, dst, sent_sem.at[0], sem, z, x, c).wait_recv()

    def left(src, on):
        remote(src, src, sent_sem.at[on], part_recv, z, x, c).wait_send()

    def a_forward(zz, dx, cc):
        piece = a_arr.at[zz, x, cc]
        return remote(piece, piece, sent_sem.at[2], a_side.at[zz], z, beside(dx), c)

    def b_forward(zz, dx):
        piece = b_arr.at[zz, x]
        return remote(piece, piece, sent_sem.at[3], b_recv.at[zz, 1], z, beside(dx), c)

    def products(zz, arr, mat, cols, blocks, acc, first):
        for xx in range(n_cell):
            for j in range(local):
                mat[zz, xx * local + j] = arr(xx, j)
        for r in range(local):
            left = jnp.concatenate([mat[zz, cols[r, k, zz]] for k in range(2)], axis=1)
            right = jnp.concatenate([blocks[r, zz, k] for k in range(2)], axis=1)
            term = dot(left, right, NT)
            if first:
                acc[r] = term
            else:
                acc[r] += term

    def a_products(zz, first):
        def arr(xx, j):
            return a_arr[zz, xx, :, :, j].reshape(2 * rows, 128)

        products(zz, arr, a_mat, a_cols, a_blocks, a_acc, first)

    def b_products(zz, first):
        def arr(xx, j):
            return b_arr[zz, xx, :, j].reshape(rows, 128)

        products(zz, arr, b_mat, b_cols, b_blocks, b_acc, first)

    def a_pass_on(zz):
        for cc in (1, 0):
            landed(a_arr.at[zz, x, cc], a_recv.at[zz, cc])
            for dx in hops:
                a_forward(zz, dx, cc).start()

    def b_pass_on(zz):
        landed(b_arr.at[zz, x], b_recv.at[zz, 0])

        @pl.when(jnp.logical_not(first_last(zz)))
        def _():
            for dx in hops:
                b_forward(zz, dx).start()

    others = beside(1) if n_cell == 2 else pl.ds(0, n_cell - 1)

    def a_take(zz, first=False):
        landed(a_arr.at[zz, others], a_side.at[zz])
        a_products(zz, first)

    def b_take(zz, first=False):
        landed(b_arr.at[zz, others], b_recv.at[zz, 1])
        b_products(zz, first)

    def phi_copy(dx, cc):
        return remote(
            phi_out.at[cc], phi_in.at[x], sent_sem.at[4 if dx else 5], phi_recv.at[min(dx, 1)],
            z, beside(dx), cc)

    @pl.when(c == 1)
    def _():
        other_layers(a_pass_on, True)
        for one in core_loads:
            one.wait()
        landed(a_arr.at[z, x, 0], a_recv.at[z, 0])
        a_take(z, True)
        other_layers(b_pass_on, True)
        other_layers(a_take, True)
        phi = jnp.concatenate([a_acc[r] for r in range(local)], axis=1).astype(jnp.bfloat16)
        phi_out[0] = phi[:rows]
        for dx in hops:
            phi_copy(dx, 0).start()
        phi_out[1] = phi[rows:]
        for dx in hops:
            phi_copy(dx, 1).start()
        phi_copy(0, 0).start()
        phi_in[x] = phi[rows:]

    @pl.when(c == 0)
    def _():
        other_layers(b_pass_on, True)

    for one in late_loads:
        one.wait()
    b_take(z, True)
    other_layers(b_take, True)

    landed(part_in.at[pl.ds(1, n_cell - 1)], part_recv)
    for dx in hops:
        panel += part_in[dx].astype(jnp.float32)
    panel_out[...] = panel.reshape(panel_out.shape)

    turned = quarter_turn(jnp.concatenate([b_acc[r] for r in range(local)], axis=1))
    cell = resist[...] * i32 + omega * turned
    left(b_arr.at[pl.ds(0, n_blk - 1), pl.ds(0, 2)], 0)
    left(a_arr.at[0, pl.ds(0, n_cell - 1)], 1)
    left(part_out.at[pl.ds(1, n_cell - 1)], 6)
    straight = (z == 0) & (c == 0) & (n_blk > 1)
    pl.when(jnp.logical_not(straight))(
        lambda: left(b_arr.at[pl.ds(0, n_blk - 1), pl.ds(0, n_cell - 1)], 3))
    if n_blk > 2:
        pl.when(straight)(lambda: left(b_arr.at[pl.ds(0, n_blk - 2), pl.ds(0, n_cell - 1)], 3))
    pl.when(c == 1)(lambda: left(a_arr.at[pl.ds(0, n_blk - 1), pl.ds(0, n_cell - 1)], 2))
    pl.when(last_first)(lambda: left(b_arr.at[0], 2))
    pl.when((c == 0) & jnp.logical_not(last_first))(lambda: left(b_arr.at[0, 0], 2))

    pl.when(c == 0)(lambda: landed(phi_in.at[x], phi_recv.at[0]))
    cell += dot(phi_in[x], inc_of(x), NN)
    landed(phi_in.at[others], phi_recv.at[1])
    for dx in hops:
        cell += dot(phi_in[beside(dx)], inc_of(beside(dx)), NN)
    cell_out[...] = cell.reshape(cell_out.shape)

    @pl.when(c == 1)
    def _():
        left(phi_out.at[0], 5)
        left(a_arr.at[0, pl.ds(0, n_cell - 1)], 4)


def per_device(p_blocks, p_cols, l_blocks, l_cols, charges, currents, omegas, resist, branch_ends):
    n_blk, n_cell = lax.axis_size("blk"), lax.axis_size("cell")
    freqs, _, share = charges.shape
    rows, local = 2 * freqs, share // 128
    vmem, dma = pltpu.VMEM, pltpu.SemaphoreType.DMA

    def by_block(v):
        return v.reshape(freqs, 2, local, 128).transpose(0, 2, 1, 3)

    operands = (
        by_block(charges), by_block(currents), branch_ends, resist.reshape(1, share), omegas,
        p_cols.transpose(0, 2, 1), l_cols.transpose(0, 2, 1), p_blocks, l_blocks,
    )
    own = (freqs, local, 2, 128)
    bf16, f32 = jnp.bfloat16, jnp.float32
    outs = pl.pallas_call(
        functools.partial(kernel, n_blk, n_cell),
        out_shape=pltpu.VMEM((2, freqs, 2, share), f32),
        in_specs=[pl.BlockSpec(memory_space=pltpu.HBM)] * len(operands),
        out_specs=pl.BlockSpec(memory_space=vmem),
        scratch_shapes=[
            vmem((n_blk, n_cell, 2) + own, bf16),
            vmem((n_blk, n_cell) + own, bf16),
            vmem((n_blk, n_cell * local, 2 * rows, 128), bf16),
            vmem((n_blk, n_cell * local, rows, 128), bf16),
            vmem(branch_ends.shape, jnp.int32),
            vmem((1, share), f32),
            pltpu.SMEM(omegas.shape, f32),
            pltpu.SMEM((local, 2, n_blk), jnp.int32),
            pltpu.SMEM((local, 2, n_blk), jnp.int32),
            vmem(p_blocks.shape, bf16),
            vmem(l_blocks.shape, bf16),
            vmem((local, 2 * rows, 128), f32),
            vmem((local, rows, 128), f32),
            vmem((n_cell * share, share), bf16),
            vmem((2, rows, share), bf16),
            vmem((n_cell, rows, share), bf16),
            vmem((n_cell, rows, share), bf16),
            vmem((n_cell, rows, share), bf16),
            dma((9,)), dma((n_blk, 2)), dma((n_blk,)), dma((n_blk, 2)), dma((7,)), dma((2,)), dma,
            pltpu.SemaphoreType.REGULAR((n_blk,)),
            pltpu.SemaphoreType.REGULAR((n_cell,)),
        ],
        compiler_params=pltpu.CompilerParams(
            collective_id=0, has_side_effects=True, vmem_limit_bytes=60 * 2**20
        ),
    )(*[pltpu.with_memory_space_constraint(v, pltpu.HBM) for v in operands])
    return outs[0], outs[1]


def solution(mesh):
    across = ("job", "blk", "cell")
    placed = (
        P(across, None, None, None, None),
        P(across, None, None),
        P(across, None, None, None, None),
        P(across, None, None),
        P("col", None, across),
        P("col", None, across),
        P("col"),
        P(across),
        P(None, across),
    )
    return jax.shard_map(
        per_device,
        mesh=mesh,
        in_specs=placed,
        out_specs=(P("col", None, across), P("col", None, across)),
        check_vma=False,
    )
```

```python
import functools

import jax
import jax.numpy as jnp
from jax import lax
from jax.experimental import pallas as pl
from jax.experimental.pallas import tpu as pltpu
from jax.sharding import PartitionSpec as P

MESH = pl.DeviceIdType.MESH
NT = (((1,), (1,)), ((), ()))
NN = (((1,), (0,)), ((), ()))


def dot(a, b, dims):
    return lax.dot_general(a, b, dims, preferred_element_type=jnp.float32)


def quarter_turn(x):
    rows = x.shape[0]
    even = lax.broadcasted_iota(jnp.int32, x.shape, 0) % 2 == 0
    return jnp.where(even, -pltpu.roll(x, rows - 1, 0), pltpu.roll(x, 1, 0))


def kernel(n_blk, n_cell, *refs):
    (charges, currents, ends_hbm, resist_hbm, omegas_hbm, p_cols, l_cols, p_blocks, l_blocks,
     both, a_arr, b_arr, a_mat, b_mat, ends, resist, omegas, a_cols, b_cols,
     a_blocks, b_blocks, a_acc, b_acc, inc, phi_out, phi_in, part_out, part_in, load_sem,
     a_recv, a_side, b_recv, sent_sem, ready, ready_beside) = refs
    cell_out, panel_out = both.at[0], both.at[1]
    freqs, local = charges.shape[0], charges.shape[1]
    rows, share = 2 * freqs, local * 128
    z, x, c = lax.axis_index("blk"), lax.axis_index("cell"), lax.axis_index("col")
    hops = range(1, n_cell)

    def beside(dx):
        return lax.rem(x + dx, n_cell)

    def remote(src, dst, send, recv, zz, xx, cc):
        return pltpu.make_async_remote_copy(
            src_ref=src, dst_ref=dst, send_sem=send, recv_sem=recv,
            device_id={"blk": zz, "cell": xx, "col": cc}, device_id_type=MESH)

    def other_layers(step, nearest):
        def at(t, carry):
            dist = t if nearest else n_blk - t
            pl.when(z >= dist)(lambda: step(z - dist))
            pl.when(z + dist < n_blk)(lambda: step(z + dist))
            return carry

        lax.fori_loop(1, n_blk, at, 0)

    barrier = pltpu.get_barrier_semaphore()

    def greet(zz, xx, cc):
        pl.semaphore_signal(
            barrier, device_id={"blk": zz, "cell": xx, "col": cc}, device_id_type=MESH)

    def loop(first, last, step):
        def at(t, carry):
            step(t)
            return carry

        lax.fori_loop(first, last, at, 0)

    def layers_below(step):
        loop(0, z, step)

    def layers_above(step):
        loop(z + 1, n_blk, step)

    def greet_chip(zz, xx):
        greet(zz, xx, 0)
        greet(zz, xx, 1)

    greet(z, x, 1 - c)
    loop(x + 1, n_cell, lambda xx: greet_chip(z, xx))
    layers_above(lambda zz: greet_chip(zz, x))

    def first_last(zz):
        return (zz == n_blk - 1) & (z == 0) & (c == 0) & (n_blk > 1)

    last_first = (z == n_blk - 1) & (c == 0) & (n_blk > 1)

    @pl.when((z == 0) & (c == 1) & (n_blk > 1))
    def _():
        for dx in hops:
            greet(n_blk - 1, beside(dx), 0)


    def load(i, src, dst):
        return pltpu.make_async_copy(src, dst, load_sem.at[i])

    loads = [
        load(0, charges, a_arr.at[z, x, c]), load(8, currents, b_arr.at[z, x]),
        load(1, ends_hbm, ends), load(2, resist_hbm, resist), load(3, omegas_hbm, omegas),
        load(4, l_cols, b_cols),
    ]
    late_loads = [load(5, l_blocks, b_blocks)]
    core_loads = [load(6, p_cols, a_cols), load(7, p_blocks, a_blocks)]

    pl.semaphore_wait(barrier, 1 + 2 * (x + z) + jnp.where(last_first, n_cell - 1, 0))

    def a_copy(zz, xx, on):
        arrives = a_side.at[z] if on == 1 else a_recv.at[z, c]
        return remote(charges, a_arr.at[z, x, c], sent_sem.at[on], arrives, zz, xx, 1)

    def ends_here(zz):
        return (zz == n_blk - 1) & (z == 0) & (n_blk > 1)

    def a_straight(xx):
        return remote(charges, a_arr.at[z, x, c], sent_sem.at[2], a_side.at[z], 0, xx, 1)

    def b_copy(zz, xx, on):
        return remote(
            currents, b_arr.at[z, x], sent_sem.at[on], b_recv.at[z, min(on, 1)], zz, xx, c)

    def answer(zz):
        def tell(cc):
            pl.semaphore_signal(
                ready.at[z - 1], device_id={"blk": zz, "cell": x, "col": cc}, device_id_type=MESH)

        tell(0)
        pl.when(c == 1)(lambda: tell(1))

    def answer_beside(xx):
        for cc in range(2):
            pl.semaphore_signal(
                ready_beside.at[x - 1], device_id={"blk": z, "cell": xx, "col": cc}, device_id_type=MESH)

    def send(zz, xx, on):
        a_copy(zz, xx, on).start()
        b_copy(zz, xx, on).start()

    layers_below(answer)
    pl.when(z > 0)(lambda: send(0, x, 0))

    @pl.when(last_first)
    def _():
        for dx in hops:
            a_straight(beside(dx)).start()

    loop(0, x, answer_beside)
    loop(0, x, lambda xx: send(z, xx, 1))
    pl.when(c == 0)(lambda: a_copy(z, x, 2).start())

    for one in loads + late_loads:
        one.start()

    @pl.when(c == 1)
    def _():
        for one in core_loads:
            one.start()

    for one in loads:
        one.wait()

    def flat(ref):
        return jnp.concatenate(
            [ref[:, j].astype(jnp.float32).reshape(rows, 128) for j in range(local)], axis=1)

    i32 = flat(b_arr.at[z, x])
    i16 = i32.astype(jnp.bfloat16)
    start = ends[0:1, :]
    stop = ends[1:2, :]
    chunk = 128
    base = lax.broadcasted_iota(jnp.int32, (chunk, share), 0)

    def fill(t, carry):
        offset = pl.multiple_of(t * chunk, chunk)
        plus = jnp.where(base == start - offset, 1.0, 0.0)
        minus = jnp.where(base == stop - offset, 1.0, 0.0)
        inc[pl.ds(offset, chunk), :] = (plus - minus).astype(jnp.bfloat16)
        return carry

    lax.fori_loop(0, n_cell * share // chunk, fill, 0)

    loop(1, z, lambda zz: a_copy(zz, x, 0).start())
    loop(1, z, lambda zz: b_copy(zz, x, 0).start())

    def inc_of(owner):
        return inc[pl.ds(pl.multiple_of(owner * share, share), share), :]

    def send_beside(xx):
        pl.semaphore_wait(ready_beside.at[xx - 1], 2)
        send(z, xx, 1)

    loop(x + 1, n_cell, send_beside)

    def part_copy(dx):
        return remote(
            part_out.at[dx], part_in.at[dx], load_sem.at[0], a_recv.at[z, 1], z, beside(dx), c)

    def send_up(zz):
        pl.semaphore_wait(ready.at[zz - 1], 2 - c)
        a_copy(zz, x, 0).start()
        pl.when((zz == n_blk - 1) | (zz == z + 1))(lambda: b_copy(zz, x, 0).start())

    layers_above(send_up)
    loop(z + 2, n_blk - 1, lambda zz: b_copy(zz, x, 0).start())

    for dx in hops:
        part_out[dx] = dot(i16, inc_of(beside(dx)), NT).astype(jnp.bfloat16)
        part_copy(dx).start()

    outflow = dot(i16, inc_of(x), NT)
    row = lax.broadcasted_iota(jnp.int32, (rows, 128), 0) // 2
    omega = jnp.zeros((rows, 128), jnp.float32)
    for f in range(freqs):
        omega = jnp.where(row == f, omegas[f], omega)
    omega = jnp.concatenate([omega] * local, axis=1)
    panel = outflow + omega * quarter_turn(flat(a_arr.at[z, x, c]))

    def landed(dst, sem):
        remote(dst, dst, sent_sem.at[0], sem, z, x, c).wait_recv()

    def left(src, sem):
        remote(src, src, sem, a_recv.at[z, 1], z, x, c).wait_send()

    def a_forward(zz, dx, cc, sem):
        piece = a_arr.at[zz, x, cc]
        return remote(piece, piece, sem, a_side.at[zz], z, beside(dx), c)

    def b_forward(zz, dx):
        piece = b_arr.at[zz, x]
        return remote(piece, piece, load_sem.at[3], b_recv.at[zz, 1], z, beside(dx), c)

    def products(zz, arr, mat, cols, blocks, acc, first):
        for xx in range(n_cell):
            for j in range(local):
                mat[zz, xx * local + j] = arr(xx, j)
        for r in range(local):
            left = jnp.concatenate([mat[zz, cols[r, k, zz]] for k in range(2)], axis=1)
            right = jnp.concatenate([blocks[r, zz, k] for k in range(2)], axis=1)
            term = dot(left, right, NT)
            if first:
                acc[r] = term
            else:
                acc[r] += term

    def a_products(zz, first):
        def arr(xx, j):
            return a_arr[zz, xx, :, :, j].reshape(2 * rows, 128)

        products(zz, arr, a_mat, a_cols, a_blocks, a_acc, first)

    def b_products(zz, first):
        def arr(xx, j):
            return b_arr[zz, xx, :, j].reshape(rows, 128)

        products(zz, arr, b_mat, b_cols, b_blocks, b_acc, first)

    def a_pass_on(zz):
        for cc in (1, 0):
            landed(a_arr.at[zz, x, cc], a_recv.at[zz, cc])

            @pl.when(jnp.logical_not(ends_here(zz)))
            def _(cc=cc):
                for dx in hops:
                    a_forward(zz, dx, cc, sent_sem.at[2]).start()

            if cc:
                @pl.when(ends_here(zz))
                def _(cc=cc):
                    for dx in hops:
                        a_forward(zz, dx, cc, load_sem.at[4]).start()

    def b_pass_on(zz):
        landed(b_arr.at[zz, x], b_recv.at[zz, 0])

        for dx in hops:
            b_forward(zz, dx).start()

    others = beside(1) if n_cell == 2 else pl.ds(0, n_cell - 1)

    def a_take(zz, first=False):
        landed(a_arr.at[zz, others], a_side.at[zz])
        a_products(zz, first)

    def b_take(zz, first=False):
        landed(b_arr.at[zz, others], b_recv.at[zz, 1])
        b_products(zz, first)

    def phi_copy(dx, cc):
        return remote(
            phi_out.at[cc], phi_in.at[x], load_sem.at[1 if dx else 2],
            b_recv.at[z, 0] if dx else a_recv.at[z, 0], z, beside(dx), cc)

    @pl.when(c == 1)
    def _():
        other_layers(a_pass_on, True)
        for one in core_loads:
            one.wait()
        landed(a_arr.at[z, x, 0], a_recv.at[z, 0])
        a_take(z, True)
        other_layers(b_pass_on, True)
        other_layers(a_take, True)
        phi = jnp.concatenate([a_acc[r] for r in range(local)], axis=1).astype(jnp.bfloat16)
        phi_out[0] = phi[:rows]
        for dx in hops:
            phi_copy(dx, 0).start()
        phi_out[1] = phi[rows:]
        for dx in hops:
            phi_copy(dx, 1).start()
        phi_copy(0, 0).start()
        phi_in[x] = phi[rows:]

    @pl.when(c == 0)
    def _():
        other_layers(b_pass_on, True)

    for one in late_loads:
        one.wait()
    b_take(z, True)
    other_layers(b_take, True)

    landed(part_in.at[pl.ds(1, n_cell - 1)], a_recv.at[z, 1])
    for dx in hops:
        panel += part_in[dx].astype(jnp.float32)
    panel_out[...] = panel.reshape(panel_out.shape)

    turned = quarter_turn(jnp.concatenate([b_acc[r] for r in range(local)], axis=1))
    cell = resist[...] * i32 + omega * turned
    left(b_arr.at[pl.ds(0, n_blk - 1), pl.ds(0, 2)], sent_sem.at[0])
    left(a_arr.at[0, pl.ds(0, n_cell - 1)], sent_sem.at[1])
    left(part_out.at[pl.ds(1, n_cell - 1)], load_sem.at[0])
    straight = z < 0
    pl.when(jnp.logical_not(straight))(
        lambda: left(b_arr.at[pl.ds(0, n_blk - 1), pl.ds(0, n_cell - 1)], load_sem.at[3]))
    if n_blk > 2:
        pl.when(straight)(lambda: left(b_arr.at[pl.ds(0, n_blk - 2), pl.ds(0, n_cell - 1)], load_sem.at[3]))
    pl.when((c == 1) & (z > 0))(
        lambda: left(a_arr.at[pl.ds(0, n_blk - 1), pl.ds(0, n_cell - 1)], sent_sem.at[2]))

    @pl.when((c == 1) & (z == 0))
    def _():
        if n_blk > 2:
            left(a_arr.at[pl.ds(0, n_blk - 2), pl.ds(0, n_cell - 1)], sent_sem.at[2])
        left(b_arr.at[0, pl.ds(0, n_cell - 1)], load_sem.at[4])

    pl.when(last_first)(lambda: left(b_arr.at[0], sent_sem.at[2]))
    pl.when((c == 0) & jnp.logical_not(last_first))(lambda: left(b_arr.at[0, 0], sent_sem.at[2]))

    pl.when(c == 0)(lambda: landed(phi_in.at[x], a_recv.at[z, 0]))
    cell += dot(phi_in[x], inc_of(x), NN)
    landed(phi_in.at[others], b_recv.at[z, 0])
    for dx in hops:
        cell += dot(phi_in[beside(dx)], inc_of(beside(dx)), NN)
    cell_out[...] = cell.reshape(cell_out.shape)

    @pl.when(c == 1)
    def _():
        left(phi_out.at[0], load_sem.at[2])
        left(a_arr.at[0, pl.ds(0, n_cell - 1)], load_sem.at[1])


def per_device(p_blocks, p_cols, l_blocks, l_cols, charges, currents, omegas, resist, branch_ends):
    n_blk, n_cell = lax.axis_size("blk"), lax.axis_size("cell")
    freqs, _, share = charges.shape
    rows, local = 2 * freqs, share // 128
    vmem, dma = pltpu.VMEM, pltpu.SemaphoreType.DMA

    def by_block(v):
        return v.reshape(freqs, 2, local, 128).transpose(0, 2, 1, 3)

    operands = (
        by_block(charges), by_block(currents), branch_ends, resist.reshape(1, share), omegas,
        p_cols.transpose(0, 2, 1), l_cols.transpose(0, 2, 1), p_blocks, l_blocks,
    )
    own = (freqs, local, 2, 128)
    bf16, f32 = jnp.bfloat16, jnp.float32
    outs = pl.pallas_call(
        functools.partial(kernel, n_blk, n_cell),
        out_shape=pltpu.VMEM((2, freqs, 2, share), f32),
        in_specs=[pl.BlockSpec(memory_space=pltpu.HBM)] * len(operands),
        out_specs=pl.BlockSpec(memory_space=vmem),
        scratch_shapes=[
            vmem((n_blk, n_cell, 2) + own, bf16),
            vmem((n_blk, n_cell) + own, bf16),
            vmem((n_blk, n_cell * local, 2 * rows, 128), bf16),
            vmem((n_blk, n_cell * local, rows, 128), bf16),
            vmem(branch_ends.shape, jnp.int32),
            vmem((1, share), f32),
            pltpu.SMEM(omegas.shape, f32),
            pltpu.SMEM((local, 2, n_blk), jnp.int32),
            pltpu.SMEM((local, 2, n_blk), jnp.int32),
            vmem(p_blocks.shape, bf16),
            vmem(l_blocks.shape, bf16),
            vmem((local, 2 * rows, 128), f32),
            vmem((local, rows, 128), f32),
            vmem((n_cell * share, share), bf16),
            vmem((2, rows, share), bf16),
            vmem((n_cell, rows, share), bf16),
            vmem((n_cell, rows, share), bf16),
            vmem((n_cell, rows, share), bf16),
            dma((9,)), dma((n_blk, 2)), dma((n_blk,)), dma((n_blk, 2)), dma((3,)),
            pltpu.SemaphoreType.REGULAR((max(n_blk - 1, 1),)),
            pltpu.SemaphoreType.REGULAR((max(n_cell - 1, 1),)),
        ],
        compiler_params=pltpu.CompilerParams(
            collective_id=0, has_side_effects=True, vmem_limit_bytes=60 * 2**20
        ),
    )(*[pltpu.with_memory_space_constraint(v, pltpu.HBM) for v in operands])
    return outs[0], outs[1]


def solution(mesh):
    across = ("job", "blk", "cell")
    placed = (
        P(across, None, None, None, None),
        P(across, None, None),
        P(across, None, None, None, None),
        P(across, None, None),
        P("col", None, across),
        P("col", None, across),
        P("col"),
        P(across),
        P(None, across),
    )
    return jax.shard_map(
        per_device,
        mesh=mesh,
        in_specs=placed,
        out_specs=(P("col", None, across), P("col", None, across)),
        check_vma=False,
    )
```

```python
import functools

import jax
import jax.numpy as jnp
from jax import lax
from jax.experimental import pallas as pl
from jax.experimental.pallas import tpu as pltpu
from jax.sharding import PartitionSpec as P

MESH = pl.DeviceIdType.MESH
NT = (((1,), (1,)), ((), ()))
NN = (((1,), (0,)), ((), ()))


def dot(a, b, dims):
    return lax.dot_general(a, b, dims, preferred_element_type=jnp.float32)


def quarter_turn(x):
    rows = x.shape[0]
    even = lax.broadcasted_iota(jnp.int32, x.shape, 0) % 2 == 0
    return jnp.where(even, -pltpu.roll(x, rows - 1, 0), pltpu.roll(x, 1, 0))


def kernel(n_blk, n_cell, *refs):
    (charges, currents, ends_hbm, resist_hbm, omegas_hbm, p_cols, l_cols, p_blocks, l_blocks,
     both, a_arr, b_arr, a_mat, b_mat, ends, resist, omegas, a_cols, b_cols,
     a_blocks, b_blocks, a_acc, b_acc, inc, phi_out, phi_in, part_out, part_in, load_sem,
     a_recv, a_side, b_recv, sent_sem, ready, ready_beside) = refs
    cell_out, panel_out = both.at[0], both.at[1]
    freqs, local = charges.shape[0], charges.shape[1]
    rows, share = 2 * freqs, local * 128
    z, x, c = lax.axis_index("blk"), lax.axis_index("cell"), lax.axis_index("col")
    hops = range(1, n_cell)

    def beside(dx):
        return lax.rem(x + dx, n_cell)

    def remote(src, dst, send, recv, zz, xx, cc):
        return pltpu.make_async_remote_copy(
            src_ref=src, dst_ref=dst, send_sem=send, recv_sem=recv,
            device_id={"blk": zz, "cell": xx, "col": cc}, device_id_type=MESH)

    def other_layers(step, nearest):
        def at(t, carry):
            dist = t if nearest else n_blk - t
            pl.when(z >= dist)(lambda: step(z - dist))
            pl.when(z + dist < n_blk)(lambda: step(z + dist))
            return carry

        lax.fori_loop(1, n_blk, at, 0)

    barrier = pltpu.get_barrier_semaphore()

    def greet(zz, xx, cc):
        pl.semaphore_signal(
            barrier, device_id={"blk": zz, "cell": xx, "col": cc}, device_id_type=MESH)

    def loop(first, last, step):
        def at(t, carry):
            step(t)
            return carry

        lax.fori_loop(first, last, at, 0)

    def layers_below(step):
        loop(0, z, step)

    def layers_above(step):
        loop(z + 1, n_blk, step)

    def greet_chip(zz, xx):
        greet(zz, xx, 0)
        greet(zz, xx, 1)

    greet(z, x, 1 - c)
    loop(x + 1, n_cell, lambda xx: greet_chip(z, xx))
    layers_above(lambda zz: greet_chip(zz, x))

    def first_last(zz):
        return (zz == n_blk - 1) & (z == 0) & (c == 0) & (n_blk > 1)

    last_first = (z == n_blk - 1) & (c == 0) & (n_blk > 1)

    @pl.when((z == 0) & (c == 1) & (n_blk > 1))
    def _():
        for dx in hops:
            greet(n_blk - 1, beside(dx), 0)


    def load(i, src, dst):
        return pltpu.make_async_copy(src, dst, load_sem.at[i])

    loads = [
        load(0, charges, a_arr.at[z, x, c]), load(8, currents, b_arr.at[z, x]),
        load(1, ends_hbm, ends), load(2, resist_hbm, resist), load(3, omegas_hbm, omegas),
        load(4, l_cols, b_cols),
    ]
    late_loads = [load(5, l_blocks, b_blocks)]
    core_loads = [load(6, p_cols, a_cols), load(7, p_blocks, a_blocks)]

    pl.semaphore_wait(barrier, 1 + 2 * (x + z) + jnp.where(last_first, n_cell - 1, 0))

    def a_copy(zz, xx, on):
        arrives = a_side.at[z] if on == 1 else a_recv.at[z, c]
        return remote(charges, a_arr.at[z, x, c], sent_sem.at[on], arrives, zz, xx, 1)

    def ends_here(zz):
        return (zz == n_blk - 1) & (z == 0) & (n_blk > 1)

    def a_straight(xx):
        return remote(charges, a_arr.at[z, x, c], sent_sem.at[2], a_side.at[z], 0, xx, 1)

    def b_copy(zz, xx, on):
        return remote(
            currents, b_arr.at[z, x], sent_sem.at[on], b_recv.at[z, min(on, 1)], zz, xx, c)

    def answer(zz):
        def tell(cc):
            pl.semaphore_signal(
                ready.at[z - 1], device_id={"blk": zz, "cell": x, "col": cc}, device_id_type=MESH)

        tell(0)
        pl.when(c == 1)(lambda: tell(1))

    def answer_beside(xx):
        for cc in range(2):
            pl.semaphore_signal(
                ready_beside.at[x - 1], device_id={"blk": z, "cell": xx, "col": cc}, device_id_type=MESH)

    def send(zz, xx, on):
        a_copy(zz, xx, on).start()
        b_copy(zz, xx, on).start()

    pl.when(z > 0)(lambda: a_copy(0, x, 0).start())

    @pl.when(last_first)
    def _():
        for dx in hops:
            a_straight(beside(dx)).start()

    pl.when(z > 0)(lambda: b_copy(0, x, 0).start())
    layers_below(answer)

    loop(0, x, answer_beside)
    loop(0, x, lambda xx: send(z, xx, 1))
    pl.when(c == 0)(lambda: a_copy(z, x, 2).start())

    for one in loads + late_loads:
        one.start()

    @pl.when(c == 1)
    def _():
        for one in core_loads:
            one.start()

    for one in loads:
        one.wait()

    def flat(ref):
        return jnp.concatenate(
            [ref[:, j].astype(jnp.float32).reshape(rows, 128) for j in range(local)], axis=1)

    i32 = flat(b_arr.at[z, x])
    i16 = i32.astype(jnp.bfloat16)
    start = ends[0:1, :]
    stop = ends[1:2, :]
    chunk = 128
    base = lax.broadcasted_iota(jnp.int32, (chunk, share), 0)

    def fill(t, carry):
        offset = pl.multiple_of(t * chunk, chunk)
        plus = jnp.where(base == start - offset, 1.0, 0.0)
        minus = jnp.where(base == stop - offset, 1.0, 0.0)
        inc[pl.ds(offset, chunk), :] = (plus - minus).astype(jnp.bfloat16)
        return carry

    lax.fori_loop(0, n_cell * share // chunk, fill, 0)

    loop(1, z, lambda zz: a_copy(zz, x, 0).start())
    loop(1, z, lambda zz: b_copy(zz, x, 0).start())

    def inc_of(owner):
        return inc[pl.ds(pl.multiple_of(owner * share, share), share), :]

    def send_beside(xx):
        pl.semaphore_wait(ready_beside.at[xx - 1], 2)
        send(z, xx, 1)

    loop(x + 1, n_cell, send_beside)

    def part_copy(dx):
        return remote(
            part_out.at[dx], part_in.at[dx], load_sem.at[0], a_recv.at[z, 1], z, beside(dx), c)

    def send_up(zz):
        pl.semaphore_wait(ready.at[zz - 1], 2 - c)
        a_copy(zz, x, 0).start()
        pl.when((zz == n_blk - 1) | (zz == z + 1))(lambda: b_copy(zz, x, 0).start())

    layers_above(send_up)
    loop(z + 2, n_blk - 1, lambda zz: b_copy(zz, x, 0).start())

    for dx in hops:
        part_out[dx] = dot(i16, inc_of(beside(dx)), NT).astype(jnp.bfloat16)
        part_copy(dx).start()

    outflow = dot(i16, inc_of(x), NT)
    row = lax.broadcasted_iota(jnp.int32, (rows, 128), 0) // 2
    omega = jnp.zeros((rows, 128), jnp.float32)
    for f in range(freqs):
        omega = jnp.where(row == f, omegas[f], omega)
    omega = jnp.concatenate([omega] * local, axis=1)
    panel = outflow + omega * quarter_turn(flat(a_arr.at[z, x, c]))

    def landed(dst, sem):
        remote(dst, dst, sent_sem.at[0], sem, z, x, c).wait_recv()

    def left(src, sem):
        remote(src, src, sem, a_recv.at[z, 1], z, x, c).wait_send()

    def a_forward(zz, dx, cc, sem):
        piece = a_arr.at[zz, x, cc]
        return remote(piece, piece, sem, a_side.at[zz], z, beside(dx), c)

    def b_forward(zz, dx):
        piece = b_arr.at[zz, x]
        return remote(piece, piece, load_sem.at[3], b_recv.at[zz, 1], z, beside(dx), c)

    def products(zz, arr, mat, cols, blocks, acc, first):
        for xx in range(n_cell):
            for j in range(local):
                mat[zz, xx * local + j] = arr(xx, j)
        for r in range(local):
            left = jnp.concatenate([mat[zz, cols[r, k, zz]] for k in range(2)], axis=1)
            right = jnp.concatenate([blocks[r, zz, k] for k in range(2)], axis=1)
            term = dot(left, right, NT)
            if first:
                acc[r] = term
            else:
                acc[r] += term

    def a_products(zz, first):
        def arr(xx, j):
            return a_arr[zz, xx, :, :, j].reshape(2 * rows, 128)

        products(zz, arr, a_mat, a_cols, a_blocks, a_acc, first)

    def b_products(zz, first):
        def arr(xx, j):
            return b_arr[zz, xx, :, j].reshape(rows, 128)

        products(zz, arr, b_mat, b_cols, b_blocks, b_acc, first)

    def a_pass_on(zz):
        for cc in (1, 0):
            landed(a_arr.at[zz, x, cc], a_recv.at[zz, cc])

            @pl.when(jnp.logical_not(ends_here(zz)))
            def _(cc=cc):
                for dx in hops:
                    a_forward(zz, dx, cc, sent_sem.at[2]).start()

            if cc:
                @pl.when(ends_here(zz))
                def _(cc=cc):
                    for dx in hops:
                        a_forward(zz, dx, cc, load_sem.at[4]).start()

    def b_pass_on(zz):
        landed(b_arr.at[zz, x], b_recv.at[zz, 0])

        for dx in hops:
            b_forward(zz, dx).start()

    others = beside(1) if n_cell == 2 else pl.ds(0, n_cell - 1)

    def a_take(zz, first=False):
        landed(a_arr.at[zz, others], a_side.at[zz])
        a_products(zz, first)

    def b_take(zz, first=False):
        landed(b_arr.at[zz, others], b_recv.at[zz, 1])
        b_products(zz, first)

    def phi_copy(dx, cc):
        return remote(
            phi_out.at[cc], phi_in.at[x], load_sem.at[1 if dx else 2],
            b_recv.at[z, 0] if dx else a_recv.at[z, 0], z, beside(dx), cc)

    @pl.when(c == 1)
    def _():
        other_layers(a_pass_on, True)
        for one in core_loads:
            one.wait()
        landed(a_arr.at[z, x, 0], a_recv.at[z, 0])
        a_take(z, True)
        other_layers(b_pass_on, True)
        other_layers(a_take, True)
        for r in range(local):
            cols = slice(r * 128, (r + 1) * 128)
            phi_out[0, :, cols] = a_acc[r, :rows].astype(jnp.bfloat16)
        for dx in hops:
            phi_copy(dx, 0).start()
        phi = jnp.concatenate([a_acc[r, rows:] for r in range(local)], axis=1).astype(jnp.bfloat16)
        phi_out[1] = phi
        for dx in hops:
            phi_copy(dx, 1).start()
        phi_copy(0, 0).start()
        phi_in[x] = phi

    @pl.when(c == 0)
    def _():
        other_layers(b_pass_on, True)

    for one in late_loads:
        one.wait()
    b_take(z, True)
    other_layers(b_take, True)

    landed(part_in.at[pl.ds(1, n_cell - 1)], a_recv.at[z, 1])
    for dx in hops:
        panel += part_in[dx].astype(jnp.float32)
    panel_out[...] = panel.reshape(panel_out.shape)

    turned = quarter_turn(jnp.concatenate([b_acc[r] for r in range(local)], axis=1))
    cell = resist[...] * i32 + omega * turned
    left(b_arr.at[pl.ds(0, n_blk - 1), pl.ds(0, 2)], sent_sem.at[0])
    left(a_arr.at[0, pl.ds(0, n_cell - 1)], sent_sem.at[1])
    left(part_out.at[pl.ds(1, n_cell - 1)], load_sem.at[0])
    straight = z < 0
    pl.when(jnp.logical_not(straight))(
        lambda: left(b_arr.at[pl.ds(0, n_blk - 1), pl.ds(0, n_cell - 1)], load_sem.at[3]))
    if n_blk > 2:
        pl.when(straight)(lambda: left(b_arr.at[pl.ds(0, n_blk - 2), pl.ds(0, n_cell - 1)], load_sem.at[3]))
    pl.when((c == 1) & (z > 0))(
        lambda: left(a_arr.at[pl.ds(0, n_blk - 1), pl.ds(0, n_cell - 1)], sent_sem.at[2]))

    @pl.when((c == 1) & (z == 0))
    def _():
        if n_blk > 2:
            left(a_arr.at[pl.ds(0, n_blk - 2), pl.ds(0, n_cell - 1)], sent_sem.at[2])
        left(b_arr.at[0, pl.ds(0, n_cell - 1)], load_sem.at[4])

    pl.when(last_first)(lambda: left(b_arr.at[0], sent_sem.at[2]))
    pl.when((c == 0) & jnp.logical_not(last_first))(lambda: left(b_arr.at[0, 0], sent_sem.at[2]))

    pl.when(c == 0)(lambda: landed(phi_in.at[x], a_recv.at[z, 0]))
    cell += dot(phi_in[x], inc_of(x), NN)
    landed(phi_in.at[others], b_recv.at[z, 0])
    for dx in hops:
        cell += dot(phi_in[beside(dx)], inc_of(beside(dx)), NN)
    cell_out[...] = cell.reshape(cell_out.shape)

    @pl.when(c == 1)
    def _():
        left(phi_out.at[0], load_sem.at[2])
        left(a_arr.at[0, pl.ds(0, n_cell - 1)], load_sem.at[1])


def per_device(p_blocks, p_cols, l_blocks, l_cols, charges, currents, omegas, resist, branch_ends):
    n_blk, n_cell = lax.axis_size("blk"), lax.axis_size("cell")
    freqs, _, share = charges.shape
    rows, local = 2 * freqs, share // 128
    vmem, dma = pltpu.VMEM, pltpu.SemaphoreType.DMA

    def by_block(v):
        return v.reshape(freqs, 2, local, 128).transpose(0, 2, 1, 3)

    operands = (
        by_block(charges), by_block(currents), branch_ends, resist.reshape(1, share), omegas,
        p_cols.transpose(0, 2, 1), l_cols.transpose(0, 2, 1), p_blocks, l_blocks,
    )
    own = (freqs, local, 2, 128)
    bf16, f32 = jnp.bfloat16, jnp.float32
    outs = pl.pallas_call(
        functools.partial(kernel, n_blk, n_cell),
        out_shape=pltpu.VMEM((2, freqs, 2, share), f32),
        in_specs=[pl.BlockSpec(memory_space=pltpu.HBM)] * len(operands),
        out_specs=pl.BlockSpec(memory_space=vmem),
        scratch_shapes=[
            vmem((n_blk, n_cell, 2) + own, bf16),
            vmem((n_blk, n_cell) + own, bf16),
            vmem((n_blk, n_cell * local, 2 * rows, 128), bf16),
            vmem((n_blk, n_cell * local, rows, 128), bf16),
            vmem(branch_ends.shape, jnp.int32),
            vmem((1, share), f32),
            pltpu.SMEM(omegas.shape, f32),
            pltpu.SMEM((local, 2, n_blk), jnp.int32),
            pltpu.SMEM((local, 2, n_blk), jnp.int32),
            vmem(p_blocks.shape, bf16),
            vmem(l_blocks.shape, bf16),
            vmem((local, 2 * rows, 128), f32),
            vmem((local, rows, 128), f32),
            vmem((n_cell * share, share), bf16),
            vmem((2, rows, share), bf16),
            vmem((n_cell, rows, share), bf16),
            vmem((n_cell, rows, share), bf16),
            vmem((n_cell, rows, share), bf16),
            dma((9,)), dma((n_blk, 2)), dma((n_blk,)), dma((n_blk, 2)), dma((3,)),
            pltpu.SemaphoreType.REGULAR((max(n_blk - 1, 1),)),
            pltpu.SemaphoreType.REGULAR((max(n_cell - 1, 1),)),
        ],
        compiler_params=pltpu.CompilerParams(
            collective_id=0, has_side_effects=True, vmem_limit_bytes=60 * 2**20
        ),
    )(*[pltpu.with_memory_space_constraint(v, pltpu.HBM) for v in operands])
    return outs[0], outs[1]


def solution(mesh):
    across = ("job", "blk", "cell")
    placed = (
        P(across, None, None, None, None),
        P(across, None, None),
        P(across, None, None, None, None),
        P(across, None, None),
        P("col", None, across),
        P("col", None, across),
        P("col"),
        P(across),
        P(None, across),
    )
    return jax.shard_map(
        per_device,
        mesh=mesh,
        in_specs=placed,
        out_specs=(P("col", None, across), P("col", None, across)),
        check_vma=False,
    )
```
